32 devices in a mesh: clip: 16 (over z, x, core), slab: 2 (over y).
Axes of the slice: x: 2, y: 2, z: 4, core: 2. Of those that a mesh axis runs over, the one named last changes fastest.
Arguments:
- frames_in: bfloat16 [32, 8, 128, 128], P('clip', 'slab')
- clip_ids: int32 [16], replicated, may hold values from 0 to 3, never falling along the last dimension, each value on 1 to 8 neighbouring positions
- gain_one: float32 [128], replicated, may hold values from 0.25 to 1.75
- shift_one: float32 [128], replicated, may hold values from -3 to 3
- kernel_one: bfloat16 [3, 3, 3, 128, 128], replicated, may hold values from -0.109375 to 0.109375
- bias_one: float32 [128], replicated, may hold values from -3 to 3
- gain_two: float32 [128], replicated, may hold values from 0.25 to 1.75
- shift_two: float32 [128], replicated, may hold values from -3 to 3
- kernel_two: bfloat16 [3, 3, 3, 128, 128], replicated, may hold values from -0.109375 to 0.109375
- bias_two: float32 [128], replicated, may hold values from -3 to 3
Outputs:
- frames_out: bfloat16 [32, 8, 128, 128], P('clip', 'slab')
The draws below stay inside these ranges and needn't reach their ends.
Inputs may be any that keep to these rules, and one draw needn't show every extreme that they name: `clip_ids`: never falling along the blocks; each clip covers 1 to 8 blocks, one exactly 8.
All inputs are finite; a program needn't handle non-finite values.
Results may differ from the reference program's by a relative error of at most 0.0075.
Values may be sent and summed in bfloat16 or wider, within the bound.
No kernel may reach another device: no remote copies, remote signals or barrier semaphores. Data moves between devices by JAX's collectives and lax.ppermute only.
A program may use at most 64 MiB of HBM per device.

```python
import math
import jax
import jax.numpy as jnp
import numpy as np
from jax import lax

C = 128
G = 32
FR_DEV = 2
ROWS = 4
W = 128
FRAMES = 32
HEIGHT = 8
CLIPS = 4
MOST = 8
N_CLIP = 16
N_SLAB = 2


def draw_frames_in(key, part):
    key_base, key_chan, key_cell, key_frame, key_row = jax.random.split(key, 5)
    shape = (FRAMES, HEIGHT, W, C)
    base = jax.random.normal(key_base, shape, jnp.float32)
    frame_order = jax.random.permutation(key_frame, FRAMES).astype(jnp.float32)
    frame_scale = 0.5 * jnp.exp(frame_order / max(FRAMES - 1, 1) * jnp.log(3.0))
    row_order = jax.random.permutation(key_row, HEIGHT).astype(jnp.float32)
    row_scale = 0.5 * jnp.exp(row_order / max(HEIGHT - 1, 1) * jnp.log(3.0))
    chan_scale = jnp.exp(jax.random.uniform(key_chan, (C,), jnp.float32, jnp.log(0.7), jnp.log(1.2)))
    cell_scale = jax.random.uniform(key_cell, (FRAMES, HEIGHT, W, 1), jnp.float32, 0.8, 1.2)
    return (base * frame_scale[:, None, None, None] * row_scale[None, :, None, None] * chan_scale * cell_scale).astype(jnp.bfloat16)


def split_up(number_of, total, most, lean):
    portions = [(1 << 20) // math.isqrt(standing ** lean) + 1 for standing in range(2, number_of + 1)]
    surplus, holding = total - most - (number_of - 1), [1] * (number_of - 1)
    while surplus > 0:
        movable = [i for i in range(number_of - 1) if holding[i] < most]
        mass, remaining = sum([portions[i] for i in movable]), surplus
        for i in movable:
            more = min(most - holding[i], max(1, remaining * portions[i] // mass), surplus)
            holding[i] = holding[i] + more
            surplus = surplus - more
    return np.array([most] + holding)


def ragged(own_key, number_of, total, reach, slope):
    if number_of == 2:
        one = jax.random.randint(own_key, (), max(1, total - reach), min(reach, total - 1) + 1)
        return jnp.stack([one, total - one])
    sizes = jnp.asarray(split_up(number_of, total, reach, slope), jnp.int32)
    couples = (number_of - 1) // 2
    source_of, sink = sizes[1:1 + 2 * couples:2], sizes[2:2 + 2 * couples:2]
    slack = jnp.minimum(source_of - 1, reach - sink)
    shifted = jax.random.randint(jax.random.fold_in(own_key, 1), (couples,), 0, 1 << 20) % (slack + 1)
    sizes = sizes.at[1:1 + 2 * couples:2].set(source_of - shifted).at[2:2 + 2 * couples:2].set(sink + shifted)
    return sizes[jax.random.permutation(jax.random.fold_in(own_key, 2), number_of)]


def gaussian(key, extent, scale, most, kind=jnp.bfloat16):
    result = scale * jax.random.normal(key, extent, jnp.float32)
    return jnp.clip(result, min=-most, max=most).astype(kind)


def setup_inputs(seed: int = 0) -> dict:
    key_of = jax.random.split(jax.random.key(seed), 11)
    return {
        "frames_in": draw_frames_in(jax.random.fold_in(key_of[10], 71), 0),
        "clip_ids": jnp.searchsorted(jnp.cumsum(ragged(key_of[1], CLIPS, N_CLIP, MOST, 2)), jnp.arange(N_CLIP), side="right").astype(jnp.int32),
        "gain_one": jnp.clip(1.0 + 0.15 * jax.random.normal(key_of[2], (C,), jnp.float32), 0.25, 1.75),
        "shift_one": gaussian(key_of[3], (C,), 0.5, 3.0, jnp.float32),
        "kernel_one": gaussian(key_of[4], (3, 3, 3, C, C), (27 * C) ** -0.5, 0.109375),
        "bias_one": gaussian(key_of[5], (C,), 0.5, 3.0, jnp.float32),
        "gain_two": jnp.clip(1.0 + 0.15 * jax.random.normal(key_of[6], (C,), jnp.float32), 0.25, 1.75),
        "shift_two": gaussian(key_of[7], (C,), 0.5, 3.0, jnp.float32),
        "kernel_two": gaussian(key_of[8], (3, 3, 3, C, C), (27 * C) ** -0.5, 0.109375),
        "bias_two": gaussian(key_of[9], (C,), 0.5, 3.0, jnp.float32),
    }


def group_act(values, frame_clip, gain, shift):
    floats = values.astype(jnp.float32)
    first = lax.optimization_barrier(jnp.sum(floats, axis=(1, 2)))
    second = lax.optimization_barrier(jnp.sum(floats * floats, axis=(1, 2)))
    onehot = (frame_clip[:, None] == jnp.arange(N_CLIP, dtype=jnp.int32)[None, :]).astype(jnp.float32)
    clip_first = jnp.dot(onehot.T, first, precision=lax.Precision.HIGHEST).reshape(N_CLIP, G, C // G).sum(2)
    clip_second = jnp.dot(onehot.T, second, precision=lax.Precision.HIGHEST).reshape(N_CLIP, G, C // G).sum(2)
    counts = jnp.maximum(lax.optimization_barrier(jnp.sum(onehot, axis=0)), 1.0) * (ROWS * N_SLAB * W * (C // G))
    mean = clip_first / counts[:, None]
    spread = clip_second / counts[:, None] - mean * mean
    inverse = lax.rsqrt(spread + 1e-06)
    mean_frame = jnp.repeat(jnp.dot(onehot, mean, precision=lax.Precision.HIGHEST), C // G, axis=1)
    inv_frame = jnp.repeat(jnp.dot(onehot, inverse, precision=lax.Precision.HIGHEST), C // G, axis=1)
    normed = (floats - mean_frame[:, None, None, :]) * inv_frame[:, None, None, :] * gain + shift
    return jax.nn.silu(normed).astype(jnp.bfloat16)

def convolve(act, frame_clip, kernel, bias):
    total_frames = act.shape[0]
    height = act.shape[1]
    width = act.shape[2]
    total = jnp.zeros((total_frames * height * width, C), jnp.float32)
    for back in range(3):
        moved = jnp.concatenate([jnp.zeros((back,) + act.shape[1:], act.dtype), act[:total_frames - back]], 0)
        valid = jnp.concatenate([jnp.zeros((back,), jnp.bool_), frame_clip[back:] == frame_clip[:total_frames - back]], 0)
        moved = moved * valid.astype(jnp.bfloat16)[:, None, None, None]
        padded = jnp.pad(moved, ((0, 0), (1, 1), (1, 1), (0, 0)))
        for row_off in range(3):
            for col_off in range(3):
                window = padded[:, row_off:row_off + height, col_off:col_off + width].reshape(-1, C)
                total = total + jnp.dot(window, kernel[2 - back, row_off, col_off], preferred_element_type=jnp.float32)
    return total.reshape(act.shape) + bias

def reference(frames_in, clip_ids, gain_one, shift_one, kernel_one, bias_one, gain_two, shift_two, kernel_two, bias_two):
    frame_clip = jnp.repeat(clip_ids, FR_DEV).astype(jnp.int32)
    act_one = group_act(frames_in, frame_clip, gain_one, shift_one)
    hidden = convolve(act_one, frame_clip, kernel_one, bias_one).astype(jnp.bfloat16)
    act_two = group_act(hidden, frame_clip, gain_two, shift_two)
    branch = convolve(act_two, frame_clip, kernel_two, bias_two)
    return (frames_in.astype(jnp.float32) + branch).astype(jnp.bfloat16)
```

```python
import functools

import jax
import jax.numpy as jnp
from jax import lax
from jax.experimental import pallas as pl
from jax.experimental.pallas import tpu as pltpu
from jax.sharding import PartitionSpec as P

G = 32
BOTH = ("clip", "slab")
EPS = 1e-06


def put_sums(floats_first, floats_second, sums_ref):
    both = jnp.concatenate([floats_first, floats_second], axis=0)
    sums_ref[...] = jnp.broadcast_to(both[None], sums_ref.shape)


def put_edges(read_row, edge_refs, slab, rows):
    if len(edge_refs) == 1:
        keep = (slab == 0).astype(jnp.float32)
        for f in range(edge_refs[0].shape[0]):
            top = read_row(f, 0).astype(jnp.float32)
            bottom = read_row(f, rows - 1).astype(jnp.float32)
            edge_refs[0][f, 0] = jnp.where(slab == 0, bottom, top).astype(jnp.bfloat16)
    else:
        for f in range(edge_refs[0].shape[0]):
            edge_refs[0][f, 0] = read_row(f, 0)
            edge_refs[1][f, 0] = read_row(f, rows - 1)


def first_kernel(frames_ref, sums_ref, *edge_refs):
    frames, rows, cols, chans = frames_ref.shape
    first = jnp.zeros((1, chans), jnp.float32)
    second = jnp.zeros((1, chans), jnp.float32)
    for f in range(frames):
        for r in range(rows):
            floats = frames_ref[f, r].astype(jnp.float32)
            first = first + jnp.sum(floats, axis=0, keepdims=True)
            second = second + jnp.sum(floats * floats, axis=0, keepdims=True)
    put_sums(first, second, sums_ref)
    put_edges(lambda f, r: frames_ref[f, r], edge_refs, lax.axis_index("slab"), rows)


def group_total(sums, per_group):
    lanes = lax.broadcasted_iota(jnp.int32, sums.shape, 1)
    width = 1
    while width < per_group:
        upper = pltpu.roll(sums, width, 1)
        lower = pltpu.roll(sums, sums.shape[1] - width, 1)
        sums = sums + jnp.where((lanes // width) % 2 == 0, lower, upper)
        width = 2 * width
    return sums


def conv_kernel(last, n_clip, n_slab, *refs):
    (ids_ref, sums_ref, own_ref, prior_ref), refs = refs[:4], refs[4:]
    count = 1 if n_slab == 2 else 2
    (up_ref, down_ref), refs = (refs[0], refs[count - 1]), refs[count:]
    (prior_up_ref, prior_down_ref), refs = (refs[0], refs[count - 1]), refs[count:]
    (gain_ref, shift_ref, bias_ref, kernel_ref), refs = refs[:4], refs[4:]
    if last:
        (residual_ref, out_ref), refs = refs[:2], refs[2:]
    else:
        (out_ref, next_sums_ref), edge_refs, refs = refs[:2], refs[2 : 2 + count], refs[2 + count :]
    act_ref = refs[0]
    frames, rows, cols, chans = own_ref.shape
    per_group = chans // G

    position = lax.axis_index("clip")
    slab = lax.axis_index("slab")
    own_clip = ids_ref[position]
    prior_clip = ids_ref[jnp.maximum(position - 1, 0)]
    same = jnp.logical_and(position > 0, prior_clip == own_clip).astype(jnp.float32)
    has_up = (slab > 0).astype(jnp.float32)
    has_down = (slab < n_slab - 1).astype(jnp.float32)

    def add_block(b, carry):
        total, blocks = carry
        weight = (ids_ref[b] == own_clip).astype(jnp.float32)
        for s in range(n_slab):
            total = total + weight * sums_ref[b * n_slab + s]
        return total, blocks + weight

    total = jnp.zeros((2, chans), jnp.float32)
    total, blocks = lax.fori_loop(0, n_clip, add_block, (total, jnp.float32(0.0)), unroll=n_clip <= 16)
    counts = blocks * float(frames * rows * n_slab * cols * per_group)
    moments = group_total(total, per_group) / counts
    mean, msq = moments[0:1], moments[1:2]
    inverse = lax.rsqrt(msq - mean * mean + EPS)
    scale = inverse * gain_ref[...]
    offset = shift_ref[...] - mean * scale
    half_scale = 0.5 * scale
    half_offset = 0.5 * offset

    def put(f, r, raw, keep=None):
        half = raw.astype(jnp.float32) * half_scale + half_offset
        act = half + half * jnp.tanh(half)
        if keep is not None:
            act = act * keep
        act_ref[f, r] = act.astype(jnp.bfloat16)

    for f in range(frames):
        put(f, 0, prior_up_ref[f, 0], same * has_up)
        put(f, rows + 1, prior_down_ref[f, 0], same * has_down)
        put(f + frames, 0, up_ref[f, 0], has_up)
        put(f + frames, rows + 1, down_ref[f, 0], has_down)
        for r in range(rows):
            put(f, r + 1, prior_ref[f, r], same)
            put(f + frames, r + 1, own_ref[f, r])

    column = lax.broadcasted_iota(jnp.int32, (rows * cols, chans), 0) % cols
    first = jnp.zeros((1, chans), jnp.float32)
    second = jnp.zeros((1, chans), jnp.float32)
    for f in range(frames):
        windows, weights = [], []
        for dt in range(3):
            for dy in range(3):
                windows.append(act_ref[f + frames - 2 + dt, dy : dy + rows].reshape(rows * cols, chans))
                weights.append(jnp.concatenate([kernel_ref[dt, dy, dx] for dx in range(3)], axis=1))
        product = jnp.dot(
            jnp.concatenate(windows, axis=1),
            jnp.concatenate(weights, axis=0),
            preferred_element_type=jnp.float32,
        )
        left = pltpu.roll(product[:, :chans], 1, 0)
        right = pltpu.roll(product[:, 2 * chans :], rows * cols - 1, 0)
        value = product[:, chans : 2 * chans] + bias_ref[...]
        value = value + jnp.where(column == 0, 0.0, left) + jnp.where(column == cols - 1, 0.0, right)
        if last:
            value = value + residual_ref[f].reshape(rows * cols, chans).astype(jnp.float32)
            out_ref[f] = value.astype(jnp.bfloat16).reshape(rows, cols, chans)
        else:
            rounded = value.astype(jnp.bfloat16)
            out_ref[f] = rounded.reshape(rows, cols, chans)
            floats = rounded.astype(jnp.float32)
            first = first + jnp.sum(floats, axis=0, keepdims=True)
            second = second + jnp.sum(floats * floats, axis=0, keepdims=True)
    if not last:
        put_sums(first, second, next_sums_ref)
        put_edges(lambda f, r: out_ref[f, r], edge_refs, slab, rows)


def exchange(values, sums, edges, n_clip, n_slab):
    def steps(dc, ds):
        return [
            (c * n_slab + s, (c + dc) * n_slab + s + ds)
            for c in range(n_clip - dc)
            for s in range(n_slab)
            if 0 <= s + ds < n_slab
        ]

    sums = lax.all_to_all(sums, BOTH, 0, 0)
    prior = lax.ppermute(values, BOTH, steps(1, 0))
    if n_slab == 2:
        beside = [lax.ppermute(edges[0], BOTH, steps(0, 1) + steps(0, -1))]
        corner = [lax.ppermute(edges[0], BOTH, steps(1, 1) + steps(1, -1))]
    else:
        top, bottom = edges
        beside = [lax.ppermute(bottom, BOTH, steps(0, 1)), lax.ppermute(top, BOTH, steps(0, -1))]
        corner = [lax.ppermute(bottom, BOTH, steps(1, 1)), lax.ppermute(top, BOTH, steps(1, -1))]
    return sums, prior, beside, corner


def per_device(
    n_clip,
    n_slab,
    frames_in,
    clip_ids,
    gain_one,
    shift_one,
    kernel_one,
    bias_one,
    gain_two,
    shift_two,
    kernel_two,
    bias_two,
):
    frames, rows, cols, chans = frames_in.shape
    count = 1 if n_slab == 2 else 2
    sums_shape = jax.ShapeDtypeStruct((n_clip * n_slab, 2, chans), jnp.float32)
    edge_shape = jax.ShapeDtypeStruct((frames, 1, cols, chans), jnp.bfloat16)
    full_shape = jax.ShapeDtypeStruct(frames_in.shape, jnp.bfloat16)
    whole = pl.BlockSpec(memory_space=pltpu.VMEM)
    table = pl.BlockSpec(memory_space=pltpu.SMEM)
    act = pltpu.VMEM((2 * frames, rows + 2, cols, chans), jnp.bfloat16)
    params = pltpu.CompilerParams(vmem_limit_bytes=24 << 20)

    def conv(last, values, sums, prior, beside, corner, gain, shift, bias, kernel, extra):
        operands = [clip_ids, sums, values, prior, *beside, *corner]
        operands += [gain[None], shift[None], bias[None], kernel, *extra]
        outs = full_shape if last else [full_shape, sums_shape] + [edge_shape] * count
        return pl.pallas_call(
            functools.partial(conv_kernel, last, n_clip, n_slab),
            out_shape=outs,
            in_specs=[table] + [whole] * (len(operands) - 1),
            out_specs=whole if last else [whole] * len(outs),
            scratch_shapes=[act],
            compiler_params=params,
            name="conv_two" if last else "conv_one",
        )(*operands)

    sums, *edges = pl.pallas_call(
        first_kernel,
        out_shape=[sums_shape] + [edge_shape] * count,
        in_specs=[whole],
        out_specs=[whole] * (1 + count),
        compiler_params=params,
        name="first_sums",
    )(frames_in)
    moved = exchange(frames_in, sums, edges, n_clip, n_slab)
    hidden, sums, *edges = conv(False, frames_in, *moved, gain_one, shift_one, bias_one, kernel_one, [])
    moved = exchange(hidden, sums, edges, n_clip, n_slab)
    return conv(True, hidden, *moved, gain_two, shift_two, bias_two, kernel_two, [frames_in])


def solution(mesh):
    placed = (P("clip", "slab", None, None), P(), P(), P(), P(), P(), P(), P(), P(), P())
    return jax.shard_map(
        functools.partial(per_device, mesh.shape["clip"], mesh.shape["slab"]),
        mesh=mesh,
        in_specs=placed,
        out_specs=P("clip", "slab", None, None),
        check_vma=False,
    )
```

```python
import functools

import jax
import jax.numpy as jnp
from jax import lax
from jax.experimental import pallas as pl
from jax.experimental.pallas import tpu as pltpu
from jax.sharding import PartitionSpec as P

G = 32
BOTH = ("clip", "slab")
EPS = 1e-06


def put_sums(first, second, sums_ref):
    both = jnp.concatenate([first, second], axis=0)
    sums_ref[...] = jnp.broadcast_to(both[None], sums_ref.shape)


def first_kernel(n_clip, n_slab, *refs):
    sources, refs = refs[:10], refs[10:]
    frames_ref, sums_ref, match_ref, table_ref, one_ref, two_ref = refs[:6]
    edge_refs, (ids_ref, param_ref, sem) = refs[6:-3], refs[-3:]
    frames_hbm, ids_hbm, gain_one, shift_one, one_hbm, bias_one, gain_two, shift_two, two_hbm, bias_two = sources
    params = [gain_one, shift_one, bias_one, gain_two, shift_two, bias_two]
    copies = [
        pltpu.make_async_copy(frames_hbm, frames_ref, sem.at[0]),
        pltpu.make_async_copy(ids_hbm, ids_ref, sem.at[1]),
        pltpu.make_async_copy(one_hbm, one_ref, sem.at[2]),
        pltpu.make_async_copy(two_hbm, two_ref, sem.at[3]),
    ]
    copies += [pltpu.make_async_copy(p, param_ref.at[i], sem.at[4 + i]) for i, p in enumerate(params)]
    for copy in copies:
        copy.start()
    frames, rows, cols, chans = frames_ref.shape
    slab = lax.axis_index("slab")
    position = lax.axis_index("clip")
    copies[0].wait()
    first = jnp.zeros((1, chans), jnp.float32)
    second = jnp.zeros((1, chans), jnp.float32)
    for f in range(frames):
        for r in range(rows):
            floats = frames_ref[f, r].astype(jnp.float32)
            first = first + jnp.sum(floats, axis=0, keepdims=True)
            second = second + jnp.sum(floats * floats, axis=0, keepdims=True)
    put_sums(first, second, sums_ref)
    if len(edge_refs) == 1:
        starts = [jnp.where(slab == 0, rows - 2, 0)]
    else:
        starts = [0, rows - 2]
    for edge_ref, start in zip(edge_refs, starts):
        for f in range(frames):
            for r in range(2):
                edge_ref[f, r] = frames_ref[f, start + r]
    copies[1].wait()
    own_clip = ids_ref[position]
    prior_clip = ids_ref[jnp.maximum(position - 1, 0)]
    same = jnp.logical_and(position > 0, prior_clip == own_clip).astype(jnp.float32)

    def add_block(b, blocks):
        weight = (ids_ref[b] == own_clip).astype(jnp.float32)
        for s in range(n_slab):
            match_ref[b * n_slab + s] = jnp.full((2, chans), weight, jnp.float32)
        return blocks + weight

    blocks = lax.fori_loop(0, n_clip, add_block, jnp.float32(0.0), unroll=n_clip <= 16)
    counts = blocks * float(frames * rows * n_slab * cols * (chans // G))
    for copy in copies[4:]:
        copy.wait()
    for i in range(len(params)):
        table_ref[i : i + 1] = param_ref[i : i + 1]
    table_ref[6:7] = jnp.full((1, chans), same, jnp.float32)
    table_ref[7:8] = jnp.full((1, chans), counts, jnp.float32)
    copies[2].wait()
    copies[3].wait()


def group_total(sums, per_group):
    lanes = lax.broadcasted_iota(jnp.int32, sums.shape, 1)
    width = 1
    while width < per_group:
        upper = pltpu.roll(sums, width, 1)
        lower = pltpu.roll(sums, sums.shape[1] - width, 1)
        sums = sums + jnp.where((lanes // width) % 2 == 0, lower, upper)
        width = 2 * width
    return sums


def half_affine(sums_ref, match_ref, table_ref, which):
    chans = table_ref.shape[1]
    total = jnp.sum(sums_ref[...] * match_ref[...], axis=0)
    moments = group_total(total, chans // G) / table_ref[7:8]
    mean, msq = moments[0:1], moments[1:2]
    scale = lax.rsqrt(msq - mean * mean + EPS) * table_ref[3 * which : 3 * which + 1]
    offset = table_ref[3 * which + 1 : 3 * which + 2] - mean * scale
    return 0.5 * scale, 0.5 * offset


def activate(raw, half_scale, half_offset):
    half = raw.astype(jnp.float32) * half_scale + half_offset
    return (half + half * jnp.tanh(half)).astype(jnp.bfloat16)


def taps(act_ref, kernel_ref, f, count):
    cols, chans = act_ref.shape[2:]
    windows, weights = [], []
    for dt in range(3):
        for dy in range(3):
            windows.append(act_ref[f + dt, dy : dy + count].reshape(count * cols, chans))
            weights.append(jnp.concatenate([kernel_ref[dt, dy, dx] for dx in range(3)], axis=1))
    product = jnp.dot(
        jnp.concatenate(windows, axis=1),
        jnp.concatenate(weights, axis=0),
        preferred_element_type=jnp.float32,
    )
    column = lax.broadcasted_iota(jnp.int32, (count * cols, chans), 0) % cols
    left = pltpu.roll(product[:, :chans], 1, 0)
    right = pltpu.roll(product[:, 2 * chans :], count * cols - 1, 0)
    left = jnp.where(column == 0, 0.0, left)
    right = jnp.where(column == cols - 1, 0.0, right)
    return product[:, chans : 2 * chans] + left + right


def conv_one_kernel(n_slab, *refs):
    (sums_ref, match_ref, table_ref, kernel_ref, own_ref, prior_ref), refs = refs[:6], refs[6:]
    count = 1 if n_slab == 2 else 2
    beside, corner, (out_ref, next_sums_ref, act_ref) = refs[:count], refs[count : 2 * count], refs[2 * count :]
    frames, rows, cols, chans = own_ref.shape
    out_rows = out_ref.shape[1]
    slab = lax.axis_index("slab")
    half_scale, half_offset = half_affine(sums_ref, match_ref, table_ref, 0)
    same = table_ref[6:7]
    empty = jnp.zeros((cols, chans), jnp.bfloat16)
    for at, body, borders, keep in ((0, prior_ref, corner, same), (frames, own_ref, beside, None)):
        scale = half_scale if keep is None else half_scale * keep
        offset = half_offset if keep is None else half_offset * keep
        for f in range(frames):
            if n_slab == 2:
                base = 1 + slab
                border = jnp.where(slab == 0, rows + 1, 0)
                act_ref[at + f, jnp.where(slab == 0, 0, rows + 2)] = empty
                for r in range(2):
                    act_ref[at + f, border + r] = activate(borders[0][f, r], scale, offset)
            else:
                base = 2
                has_up = (slab > 0).astype(jnp.float32)
                has_down = (slab < n_slab - 1).astype(jnp.float32)
                for r in range(2):
                    act_ref[at + f, r] = activate(borders[0][f, r], scale * has_up, offset * has_up)
                    act_ref[at + f, rows + 2 + r] = activate(borders[1][f, r], scale * has_down, offset * has_down)
            for r in range(rows):
                act_ref[at + f, base + r] = activate(body[f, r], scale, offset)
    first = jnp.zeros((1, chans), jnp.float32)
    second = jnp.zeros((1, chans), jnp.float32)
    own_base = slab if n_slab == 2 else 1
    for f in range(frames):
        value = taps(act_ref, kernel_ref, f, out_rows) + table_ref[2:3]
        rounded = value.astype(jnp.bfloat16).reshape(out_rows, cols, chans)
        out_ref[f] = rounded
        for r in range(out_rows):
            inside = jnp.logical_and(r >= own_base, r < own_base + rows).astype(jnp.float32)
            floats = rounded[r].astype(jnp.float32)
            first = first + inside * jnp.sum(floats, axis=0, keepdims=True)
            second = second + inside * jnp.sum(floats * floats, axis=0, keepdims=True)
    put_sums(first, second, next_sums_ref)


def conv_two_kernel(n_slab, sums_ref, match_ref, table_ref, kernel_ref, own_ref, prior_ref, residual_ref, out_ref, act_ref):
    frames, rows, cols, chans = residual_ref.shape
    slab = lax.axis_index("slab")
    half_scale, half_offset = half_affine(sums_ref, match_ref, table_ref, 1)
    same = table_ref[6:7]
    empty = jnp.zeros((cols, chans), jnp.bfloat16)
    has_up = (slab > 0).astype(jnp.float32)
    has_down = (slab < n_slab - 1).astype(jnp.float32)
    count = own_ref.shape[1]
    for at, body, keep in ((0, prior_ref, same), (frames, own_ref, None)):
        scale = half_scale if keep is None else half_scale * keep
        offset = half_offset if keep is None else half_offset * keep
        for f in range(frames):
            if n_slab == 2:
                act_ref[at + f, jnp.where(slab == 0, 0, rows + 1)] = empty
                for r in range(count):
                    act_ref[at + f, 1 - slab + r] = activate(body[f, r], scale, offset)
            else:
                for r in range(count):
                    edge = has_up if r == 0 else has_down if r == count - 1 else 1.0
                    act_ref[at + f, r] = activate(body[f, r], scale * edge, offset * edge)
    for f in range(frames):
        value = taps(act_ref, kernel_ref, f, rows) + table_ref[5:6]
        value = value + residual_ref[f].reshape(rows * cols, chans).astype(jnp.float32)
        out_ref[f] = value.astype(jnp.bfloat16).reshape(rows, cols, chans)


def per_device(n_clip, n_slab, *args):
    frames_in, kernel = args[0], args[4]
    frames, rows, cols, chans = frames_in.shape
    count = 1 if n_slab == 2 else 2
    shape = jax.ShapeDtypeStruct
    sums_shape = shape((n_clip * n_slab, 2, chans), jnp.float32)
    vmem = pl.BlockSpec(memory_space=pltpu.VMEM)
    params = pltpu.CompilerParams(vmem_limit_bytes=24 << 20)

    def steps(dc, ds):
        return [
            (c * n_slab + s, (c + dc) * n_slab + s + ds)
            for c in range(n_clip - dc)
            for s in range(n_slab)
            if 0 <= s + ds < n_slab
        ]

    def call(kernel, outs, operands, scratch, name, space=pltpu.VMEM):
        return pl.pallas_call(
            kernel,
            out_shape=outs,
            in_specs=[pl.BlockSpec(memory_space=space)] * len(operands),
            out_specs=jax.tree.map(lambda _: vmem, outs),
            scratch_shapes=scratch,
            compiler_params=params,
            name=name,
        )(*operands)

    prior = lax.ppermute(frames_in, BOTH, steps(1, 0))
    outs = [shape(frames_in.shape, frames_in.dtype), sums_shape, sums_shape, shape((8, chans), jnp.float32)]
    outs += [shape(kernel.shape, kernel.dtype)] * 2
    outs += [shape((frames, 2, cols, chans), jnp.bfloat16)] * count
    scratch = [pltpu.SMEM((n_clip,), jnp.int32), pltpu.VMEM((6, chans), jnp.float32), pltpu.SemaphoreType.DMA((10,))]
    frames_own, sums, match, table, kernel_one, kernel_two, *edges = call(
        functools.partial(first_kernel, n_clip, n_slab), outs, args, scratch, "first_sums", pltpu.HBM
    )
    if n_slab == 2:
        beside = [lax.ppermute(edges[0], BOTH, steps(0, 1) + steps(0, -1))]
        corner = [lax.ppermute(edges[0], BOTH, steps(1, 1) + steps(1, -1))]
    else:
        top, bottom = edges
        beside = [lax.ppermute(bottom, BOTH, steps(0, 1)), lax.ppermute(top, BOTH, steps(0, -1))]
        corner = [lax.ppermute(bottom, BOTH, steps(1, 1)), lax.ppermute(top, BOTH, steps(1, -1))]
    sums = lax.all_to_all(sums, BOTH, 0, 0)
    hidden, sums = call(
        functools.partial(conv_one_kernel, n_slab),
        [shape((frames, rows + count, cols, chans), jnp.bfloat16), sums_shape],
        [sums, match, table, kernel_one, frames_own, prior, *beside, *corner],
        [pltpu.VMEM((2 * frames, rows + 2 + count, cols, chans), jnp.bfloat16)],
        "conv_one",
    )
    prior = lax.ppermute(hidden, BOTH, steps(1, 0))
    sums = lax.all_to_all(sums, BOTH, 0, 0)
    return call(
        functools.partial(conv_two_kernel, n_slab),
        shape(frames_in.shape, jnp.bfloat16),
        [sums, match, table, kernel_two, hidden, prior, frames_own],
        [pltpu.VMEM((2 * frames, rows + 2, cols, chans), jnp.bfloat16)],
        "conv_two",
    )


def solution(mesh):
    placed = (P("clip", "slab", None, None), P(), P(), P(), P(), P(), P(), P(), P(), P())
    return jax.shard_map(
        functools.partial(per_device, mesh.shape["clip"], mesh.shape["slab"]),
        mesh=mesh,
        in_specs=placed,
        out_specs=P("clip", "slab", None, None),
        check_vma=False,
    )
```

```python
import functools

import jax
import jax.numpy as jnp
from jax import lax
from jax.experimental import pallas as pl
from jax.experimental.pallas import tpu as pltpu
from jax.sharding import PartitionSpec as P

G = 32
BOTH = ("clip", "slab")
EPS = 1e-06


def put_sums(first, second, sums_ref):
    both = jnp.concatenate([first, second], axis=0)
    sums_ref[...] = jnp.broadcast_to(both[None], sums_ref.shape)


def first_kernel(n_clip, n_slab, *refs):
    sources, refs = refs[:10], refs[10:]
    frames_ref, sums_ref, match_ref, table_ref, one_ref, two_ref = refs[:6]
    edge_refs, (ids_ref, param_ref, sem) = refs[6:-3], refs[-3:]
    frames_hbm, ids_hbm, gain_one, shift_one, one_hbm, bias_one, gain_two, shift_two, two_hbm, bias_two = sources
    params = [gain_one, shift_one, bias_one, gain_two, shift_two, bias_two]
    copies = [
        pltpu.make_async_copy(frames_hbm, frames_ref, sem.at[0]),
        pltpu.make_async_copy(ids_hbm, ids_ref, sem.at[1]),
        pltpu.make_async_copy(one_hbm, one_ref, sem.at[2]),
        pltpu.make_async_copy(two_hbm, two_ref, sem.at[3]),
    ]
    copies += [pltpu.make_async_copy(p, param_ref.at[i], sem.at[4 + i]) for i, p in enumerate(params)]
    for copy in copies:
        copy.start()
    frames, rows, cols, chans = frames_ref.shape
    slab = lax.axis_index("slab")
    position = lax.axis_index("clip")
    copies[0].wait()
    first = jnp.zeros((1, chans), jnp.float32)
    second = jnp.zeros((1, chans), jnp.float32)
    for f in range(frames):
        for r in range(rows):
            floats = frames_ref[f, r].astype(jnp.float32)
            first = first + jnp.sum(floats, axis=0, keepdims=True)
            second = second + jnp.sum(floats * floats, axis=0, keepdims=True)
    put_sums(first, second, sums_ref)
    if len(edge_refs) == 1:
        starts = [jnp.where(slab == 0, rows - 2, 0)]
    else:
        starts = [0, rows - 2]
    for edge_ref, start in zip(edge_refs, starts):
        for f in range(frames):
            for r in range(2):
                edge_ref[f, r] = frames_ref[f, start + r]
    copies[1].wait()
    own_clip = ids_ref[position]
    prior_clip = ids_ref[jnp.maximum(position - 1, 0)]
    same = jnp.logical_and(position > 0, prior_clip == own_clip).astype(jnp.float32)

    def add_block(b, blocks):
        weight = (ids_ref[b] == own_clip).astype(jnp.float32)
        for s in range(n_slab):
            match_ref[b * n_slab + s] = jnp.full((2, chans), weight, jnp.float32)
        return blocks + weight

    blocks = lax.fori_loop(0, n_clip, add_block, jnp.float32(0.0), unroll=n_clip <= 16)
    counts = blocks * float(frames * rows * n_slab * cols * (chans // G))
    for copy in copies[4:]:
        copy.wait()
    for i in range(len(params)):
        table_ref[i : i + 1] = param_ref[i : i + 1]
    table_ref[6:7] = jnp.full((1, chans), same, jnp.float32)
    table_ref[7:8] = jnp.full((1, chans), counts, jnp.float32)
    copies[2].wait()
    copies[3].wait()


def group_total(sums, per_group):
    lanes = lax.broadcasted_iota(jnp.int32, sums.shape, 1)
    width = 1
    while width < per_group:
        upper = pltpu.roll(sums, width, 1)
        lower = pltpu.roll(sums, sums.shape[1] - width, 1)
        sums = sums + jnp.where((lanes // width) % 2 == 0, lower, upper)
        width = 2 * width
    return sums


def half_affine(sums_ref, match_ref, table_ref, which):
    chans = table_ref.shape[1]
    total = jnp.sum(sums_ref[...] * match_ref[...], axis=0)
    moments = group_total(total, chans // G) / table_ref[7:8]
    mean, msq = moments[0:1], moments[1:2]
    scale = lax.rsqrt(msq - mean * mean + EPS) * table_ref[3 * which : 3 * which + 1]
    offset = table_ref[3 * which + 1 : 3 * which + 2] - mean * scale
    return 0.5 * scale, 0.5 * offset


def activate(raw, half_scale, half_offset):
    half = raw.astype(jnp.float32) * half_scale + half_offset
    return (half + half * jnp.tanh(half)).astype(jnp.bfloat16)


def taps(act_ref, kernel_ref, f, count):
    cols, chans = act_ref.shape[2:]
    windows, weights = [], []
    for dt in range(3):
        for dy in range(3):
            windows.append(act_ref[f + dt, dy : dy + count].reshape(count * cols, chans))
            weights.append(jnp.concatenate([kernel_ref[dt, dy, dx] for dx in range(3)], axis=1))
    product = jnp.dot(
        jnp.concatenate(windows, axis=1),
        jnp.concatenate(weights, axis=0),
        preferred_element_type=jnp.float32,
    )
    column = lax.broadcasted_iota(jnp.int32, (count * cols, chans), 0) % cols
    left = pltpu.roll(product[:, :chans], 1, 0)
    right = pltpu.roll(product[:, 2 * chans :], count * cols - 1, 0)
    left = jnp.where(column == 0, 0.0, left)
    right = jnp.where(column == cols - 1, 0.0, right)
    return product[:, chans : 2 * chans] + left + right


def conv_one_kernel(n_slab, *refs):
    (sums_ref, match_ref, table_ref, kernel_ref, own_ref, prior_ref), refs = refs[:6], refs[6:]
    count = 1 if n_slab == 2 else 2
    beside, corner, (out_ref, next_sums_ref, act_ref) = refs[:count], refs[count : 2 * count], refs[2 * count :]
    frames, rows, cols, chans = own_ref.shape
    out_rows = out_ref.shape[1]
    slab = lax.axis_index("slab")
    half_scale, half_offset = half_affine(sums_ref, match_ref, table_ref, 0)
    same = table_ref[6:7]
    empty = jnp.zeros((cols, chans), jnp.bfloat16)
    for at, body, borders, keep in ((0, prior_ref, corner, same), (frames, own_ref, beside, None)):
        scale = half_scale if keep is None else half_scale * keep
        offset = half_offset if keep is None else half_offset * keep
        for f in range(frames):
            if n_slab == 2:
                base = 1 + slab
                border = jnp.where(slab == 0, rows + 1, 0)
                act_ref[at + f, jnp.where(slab == 0, 0, rows + 2)] = empty
                for r in range(2):
                    act_ref[at + f, border + r] = activate(borders[0][f, r], scale, offset)
            else:
                base = 2
                has_up = (slab > 0).astype(jnp.float32)
                has_down = (slab < n_slab - 1).astype(jnp.float32)
                for r in range(2):
                    act_ref[at + f, r] = activate(borders[0][f, r], scale * has_up, offset * has_up)
                    act_ref[at + f, rows + 2 + r] = activate(borders[1][f, r], scale * has_down, offset * has_down)
            for r in range(rows):
                act_ref[at + f, base + r] = activate(body[f, r], scale, offset)
    first = jnp.zeros((1, chans), jnp.float32)
    second = jnp.zeros((1, chans), jnp.float32)
    own_base = slab if n_slab == 2 else 1
    for f in range(frames):
        value = taps(act_ref, kernel_ref, f, out_rows) + table_ref[2:3]
        rounded = value.astype(jnp.bfloat16).reshape(out_rows, cols, chans)
        out_ref[f] = rounded
        for r in range(out_rows):
            inside = jnp.logical_and(r >= own_base, r < own_base + rows).astype(jnp.float32)
            floats = rounded[r].astype(jnp.float32)
            first = first + inside * jnp.sum(floats, axis=0, keepdims=True)
            second = second + inside * jnp.sum(floats * floats, axis=0, keepdims=True)
    put_sums(first, second, next_sums_ref)


def conv_two_kernel(n_slab, sums_ref, match_ref, table_ref, kernel_ref, own_ref, prior_ref, residual_ref, out_ref, act_ref):
    frames, rows, cols, chans = residual_ref.shape
    slab = lax.axis_index("slab")
    half_scale, half_offset = half_affine(sums_ref, match_ref, table_ref, 1)
    same = table_ref[6:7]
    empty = jnp.zeros((cols, chans), jnp.bfloat16)
    has_up = (slab > 0).astype(jnp.float32)
    has_down = (slab < n_slab - 1).astype(jnp.float32)
    count = own_ref.shape[1]
    for at, body, keep in ((0, prior_ref, same), (frames, own_ref, None)):
        scale = half_scale if keep is None else half_scale * keep
        offset = half_offset if keep is None else half_offset * keep
        for f in range(frames):
            if n_slab == 2:
                act_ref[at + f, jnp.where(slab == 0, 0, rows + 1)] = empty
                for r in range(count):
                    act_ref[at + f, 1 - slab + r] = activate(body[f, r], scale, offset)
            else:
                for r in range(count):
                    edge = has_up if r == 0 else has_down if r == count - 1 else 1.0
                    act_ref[at + f, r] = activate(body[f, r], scale * edge, offset * edge)
    for f in range(frames):
        value = taps(act_ref, kernel_ref, f, rows) + table_ref[5:6]
        value = value + residual_ref[f].reshape(rows * cols, chans).astype(jnp.float32)
        out_ref[f] = value.astype(jnp.bfloat16).reshape(rows, cols, chans)


def per_device(n_clip, n_slab, *args):
    frames_in, kernel = args[0], args[4]
    frames, rows, cols, chans = frames_in.shape
    count = 1 if n_slab == 2 else 2
    shape = jax.ShapeDtypeStruct
    sums_shape = shape((n_clip * n_slab, 2, chans), jnp.float32)
    vmem = pl.BlockSpec(memory_space=pltpu.VMEM)
    params = pltpu.CompilerParams(vmem_limit_bytes=24 << 20)

    def steps(dc, ds):
        return [
            (c * n_slab + s, (c + dc) * n_slab + s + ds)
            for c in range(n_clip - dc)
            for s in range(n_slab)
            if 0 <= s + ds < n_slab
        ]

    def call(kernel, outs, operands, scratch, name, space=pltpu.VMEM):
        if space == pltpu.HBM:
            operands = [pltpu.with_memory_space_constraint(x, pltpu.HBM) for x in operands]
        return pl.pallas_call(
            kernel,
            out_shape=outs,
            in_specs=[pl.BlockSpec(memory_space=space)] * len(operands),
            out_specs=jax.tree.map(lambda _: vmem, outs),
            scratch_shapes=scratch,
            compiler_params=params,
            name=name,
        )(*operands)

    prior = lax.ppermute(frames_in, BOTH, steps(1, 0))
    outs = [shape(frames_in.shape, frames_in.dtype), sums_shape, sums_shape, shape((8, chans), jnp.float32)]
    outs += [shape(kernel.shape, kernel.dtype)] * 2
    outs += [shape((frames, 2, cols, chans), jnp.bfloat16)] * count
    scratch = [pltpu.SMEM((n_clip,), jnp.int32), pltpu.VMEM((6, chans), jnp.float32), pltpu.SemaphoreType.DMA((10,))]
    frames_own, sums, match, table, kernel_one, kernel_two, *edges = call(
        functools.partial(first_kernel, n_clip, n_slab), outs, args, scratch, "first_sums", pltpu.HBM
    )
    if n_slab == 2:
        beside = [lax.ppermute(edges[0], BOTH, steps(0, 1) + steps(0, -1))]
        corner = [lax.ppermute(edges[0], BOTH, steps(1, 1) + steps(1, -1))]
    else:
        top, bottom = edges
        beside = [lax.ppermute(bottom, BOTH, steps(0, 1)), lax.ppermute(top, BOTH, steps(0, -1))]
        corner = [lax.ppermute(bottom, BOTH, steps(1, 1)), lax.ppermute(top, BOTH, steps(1, -1))]
    sums = lax.all_to_all(sums, BOTH, 0, 0)
    hidden, sums = call(
        functools.partial(conv_one_kernel, n_slab),
        [shape((frames, rows + count, cols, chans), jnp.bfloat16), sums_shape],
        [sums, match, table, kernel_one, frames_own, prior, *beside, *corner],
        [pltpu.VMEM((2 * frames, rows + 2 + count, cols, chans), jnp.bfloat16)],
        "conv_one",
    )
    prior = lax.ppermute(hidden, BOTH, steps(1, 0))
    sums = lax.all_to_all(sums, BOTH, 0, 0)
    return call(
        functools.partial(conv_two_kernel, n_slab),
        shape(frames_in.shape, jnp.bfloat16),
        [sums, match, table, kernel_two, hidden, prior, frames_own],
        [pltpu.VMEM((2 * frames, rows + 2, cols, chans), jnp.bfloat16)],
        "conv_two",
    )


def solution(mesh):
    placed = (P("clip", "slab", None, None), P(), P(), P(), P(), P(), P(), P(), P(), P())
    return jax.shard_map(
        functools.partial(per_device, mesh.shape["clip"], mesh.shape["slab"]),
        mesh=mesh,
        in_specs=placed,
        out_specs=P("clip", "slab", None, None),
        check_vma=False,
    )
```

```python
import functools

import jax
import jax.numpy as jnp
from jax import lax
from jax.experimental import pallas as pl
from jax.experimental.pallas import tpu as pltpu
from jax.sharding import PartitionSpec as P

G = 32
BOTH = ("clip", "slab")
EPS = 1e-06


def put_sums(first, second, sums_ref):
    both = jnp.concatenate([first, second], axis=0)
    sums_ref[...] = jnp.broadcast_to(both[None], sums_ref.shape)


def first_kernel(n_clip, n_slab, *refs):
    sources, refs = refs[:9], refs[9:]
    frames_ref, sums_ref, match_ref, table_ref, one_ref = refs[:5]
    edge_refs, (ids_ref, param_ref, sem) = refs[5:-3], refs[-3:]
    frames_hbm, ids_hbm, gain_one, shift_one, one_hbm, bias_one, gain_two, shift_two, bias_two = sources
    params = [gain_one, shift_one, bias_one, gain_two, shift_two, bias_two]
    copies = [
        pltpu.make_async_copy(frames_hbm, frames_ref, sem.at[0]),
        pltpu.make_async_copy(ids_hbm, ids_ref, sem.at[1]),
        pltpu.make_async_copy(one_hbm, one_ref, sem.at[2]),
    ]
    copies += [pltpu.make_async_copy(p, param_ref.at[i], sem.at[3 + i]) for i, p in enumerate(params)]
    for copy in copies:
        copy.start()
    frames, rows, cols, chans = frames_ref.shape
    slab = lax.axis_index("slab")
    position = lax.axis_index("clip")
    copies[0].wait()
    first = jnp.zeros((1, chans), jnp.float32)
    second = jnp.zeros((1, chans), jnp.float32)
    for f in range(frames):
        for r in range(rows):
            floats = frames_ref[f, r].astype(jnp.float32)
            first = first + jnp.sum(floats, axis=0, keepdims=True)
            second = second + jnp.sum(floats * floats, axis=0, keepdims=True)
    put_sums(first, second, sums_ref)
    if len(edge_refs) == 1:
        starts = [jnp.where(slab == 0, rows - 2, 0)]
    else:
        starts = [0, rows - 2]
    for edge_ref, start in zip(edge_refs, starts):
        for f in range(frames):
            for r in range(2):
                edge_ref[f, r] = frames_ref[f, start + r]
    copies[1].wait()
    own_clip = ids_ref[position]
    prior_clip = ids_ref[jnp.maximum(position - 1, 0)]
    same = jnp.logical_and(position > 0, prior_clip == own_clip).astype(jnp.float32)

    def add_block(b, blocks):
        weight = (ids_ref[b] == own_clip).astype(jnp.float32)
        for s in range(n_slab):
            match_ref[b * n_slab + s] = jnp.full((2, chans), weight, jnp.float32)
        return blocks + weight

    blocks = lax.fori_loop(0, n_clip, add_block, jnp.float32(0.0), unroll=n_clip <= 16)
    counts = blocks * float(frames * rows * n_slab * cols * (chans // G))
    for copy in copies[3:]:
        copy.wait()
    for i in range(len(params)):
        table_ref[i : i + 1] = param_ref[i : i + 1]
    table_ref[6:7] = jnp.full((1, chans), same, jnp.float32)
    table_ref[7:8] = jnp.full((1, chans), counts, jnp.float32)
    copies[2].wait()


def group_total(sums, per_group):
    lanes = lax.broadcasted_iota(jnp.int32, sums.shape, 1)
    width = 1
    while width < per_group:
        upper = pltpu.roll(sums, width, 1)
        lower = pltpu.roll(sums, sums.shape[1] - width, 1)
        sums = sums + jnp.where((lanes // width) % 2 == 0, lower, upper)
        width = 2 * width
    return sums


def half_affine(sums_ref, match_ref, table_ref, which):
    chans = table_ref.shape[1]
    total = jnp.sum(sums_ref[...] * match_ref[...], axis=0)
    moments = group_total(total, chans // G) / table_ref[7:8]
    mean, msq = moments[0:1], moments[1:2]
    scale = lax.rsqrt(msq - mean * mean + EPS) * table_ref[3 * which : 3 * which + 1]
    offset = table_ref[3 * which + 1 : 3 * which + 2] - mean * scale
    return 0.5 * scale, 0.5 * offset


def activate(raw, half_scale, half_offset):
    half = raw.astype(jnp.float32) * half_scale + half_offset
    return (half + half * jnp.tanh(half)).astype(jnp.bfloat16)


def products(act_ref, kernel_ref, frames, count):
    cols, chans = act_ref.shape[2:]
    empty = jnp.zeros((chans, chans), jnp.bfloat16)

    def window(t):
        return [act_ref[t, dy : dy + count].reshape(count * cols, chans) for dy in range(3)]

    def weight(dt, dy, dx):
        return kernel_ref[dt, dy, dx] if 0 <= dt < 3 else empty

    def dot(windows, weights):
        return jnp.dot(
            jnp.concatenate(windows, axis=1), jnp.concatenate(weights, axis=0), preferred_element_type=jnp.float32
        )

    windows = [window(t) for t in range(frames + 2)]
    sides = [
        jnp.concatenate([weight(t - f, dy, 2) for f in range(frames)], axis=1)
        for t in range(frames + 2)
        for dy in range(3)
    ]
    rights = dot(sum(windows, []), sides)
    column = lax.broadcasted_iota(jnp.int32, (count * cols, chans), 0) % cols
    pairs = [jnp.concatenate([weight(dt, dy, 0), weight(dt, dy, 1)], axis=1) for dt in range(3) for dy in range(3)]
    for f in range(frames):
        product = dot(windows[f] + windows[f + 1] + windows[f + 2], pairs)
        left = pltpu.roll(product[:, :chans], 1, 0)
        right = pltpu.roll(rights[:, f * chans : (f + 1) * chans], count * cols - 1, 0)
        left = jnp.where(column == 0, 0.0, left)
        right = jnp.where(column == cols - 1, 0.0, right)
        yield f, product[:, chans:] + left + right


def conv_one_kernel(n_slab, *refs):
    (two_hbm, sums_ref, match_ref, table_ref, kernel_ref, own_ref, prior_ref), refs = refs[:7], refs[7:]
    count = 1 if n_slab == 2 else 2
    beside, corner, refs = refs[:count], refs[count : 2 * count], refs[2 * count :]
    out_ref, next_sums_ref, two_ref, act_ref, sem = refs
    fetch = pltpu.make_async_copy(two_hbm, two_ref, sem.at[0])
    fetch.start()
    frames, rows, cols, chans = own_ref.shape
    out_rows = out_ref.shape[1]
    slab = lax.axis_index("slab")
    half_scale, half_offset = half_affine(sums_ref, match_ref, table_ref, 0)
    same = table_ref[6:7]
    empty = jnp.zeros((cols, chans), jnp.bfloat16)
    for at, body, borders, keep in ((0, prior_ref, corner, same), (frames, own_ref, beside, None)):
        scale = half_scale if keep is None else half_scale * keep
        offset = half_offset if keep is None else half_offset * keep
        for f in range(frames):
            if n_slab == 2:
                base = 1 + slab
                border = jnp.where(slab == 0, rows + 1, 0)
                act_ref[at + f, jnp.where(slab == 0, 0, rows + 2)] = empty
                for r in range(2):
                    act_ref[at + f, border + r] = activate(borders[0][f, r], scale, offset)
            else:
                base = 2
                has_up = (slab > 0).astype(jnp.float32)
                has_down = (slab < n_slab - 1).astype(jnp.float32)
                for r in range(2):
                    act_ref[at + f, r] = activate(borders[0][f, r], scale * has_up, offset * has_up)
                    act_ref[at + f, rows + 2 + r] = activate(borders[1][f, r], scale * has_down, offset * has_down)
            for r in range(rows):
                act_ref[at + f, base + r] = activate(body[f, r], scale, offset)
    first = jnp.zeros((1, chans), jnp.float32)
    second = jnp.zeros((1, chans), jnp.float32)
    own_base = slab if n_slab == 2 else 1
    for f, value in products(act_ref, kernel_ref, frames, out_rows):
        value = value + table_ref[2:3]
        rounded = value.astype(jnp.bfloat16).reshape(out_rows, cols, chans)
        out_ref[f] = rounded
        for r in range(out_rows):
            inside = jnp.logical_and(r >= own_base, r < own_base + rows).astype(jnp.float32)
            floats = rounded[r].astype(jnp.float32)
            first = first + inside * jnp.sum(floats, axis=0, keepdims=True)
            second = second + inside * jnp.sum(floats * floats, axis=0, keepdims=True)
    put_sums(first, second, next_sums_ref)
    fetch.wait()


def conv_two_kernel(n_slab, sums_ref, match_ref, table_ref, kernel_ref, own_ref, prior_ref, residual_ref, out_hbm, act_ref, out_ref, sem):
    frames, rows, cols, chans = residual_ref.shape
    slab = lax.axis_index("slab")
    half_scale, half_offset = half_affine(sums_ref, match_ref, table_ref, 1)
    same = table_ref[6:7]
    empty = jnp.zeros((cols, chans), jnp.bfloat16)
    has_up = (slab > 0).astype(jnp.float32)
    has_down = (slab < n_slab - 1).astype(jnp.float32)
    count = own_ref.shape[1]
    stores = []
    for at, body, keep in ((0, prior_ref, same), (frames, own_ref, None)):
        scale = half_scale if keep is None else half_scale * keep
        offset = half_offset if keep is None else half_offset * keep
        for f in range(frames):
            if n_slab == 2:
                act_ref[at + f, jnp.where(slab == 0, 0, rows + 1)] = empty
                for r in range(count):
                    act_ref[at + f, 1 - slab + r] = activate(body[f, r], scale, offset)
            else:
                for r in range(count):
                    edge = has_up if r == 0 else has_down if r == count - 1 else 1.0
                    act_ref[at + f, r] = activate(body[f, r], scale * edge, offset * edge)
    for f, value in products(act_ref, kernel_ref, frames, rows):
        value = value + table_ref[5:6]
        value = value + residual_ref[f].reshape(rows * cols, chans).astype(jnp.float32)
        out_ref[f] = value.astype(jnp.bfloat16).reshape(rows, cols, chans)
        stores.append(pltpu.make_async_copy(out_ref.at[f], out_hbm.at[f], sem.at[f]))
        stores[-1].start()
    for store in stores:
        store.wait()


def per_device(n_clip, n_slab, *args):
    frames_in, kernel = args[0], args[4]
    frames, rows, cols, chans = frames_in.shape
    count = 1 if n_slab == 2 else 2
    shape = jax.ShapeDtypeStruct
    sums_shape = shape((n_clip * n_slab, 2, chans), jnp.float32)
    vmem = pl.BlockSpec(memory_space=pltpu.VMEM)
    hbm = pl.BlockSpec(memory_space=pltpu.HBM)
    params = pltpu.CompilerParams(vmem_limit_bytes=24 << 20)

    def steps(dc, ds):
        return [
            (c * n_slab + s, (c + dc) * n_slab + s + ds)
            for c in range(n_clip - dc)
            for s in range(n_slab)
            if 0 <= s + ds < n_slab
        ]

    def call(kernel, outs, distant, operands, scratch, name, out_spec=vmem):
        distant = [pltpu.with_memory_space_constraint(x, pltpu.HBM) for x in distant]
        operands = distant + operands
        return pl.pallas_call(
            kernel,
            out_shape=outs,
            in_specs=[hbm] * len(distant) + [vmem] * (len(operands) - len(distant)),
            out_specs=jax.tree.map(lambda _: out_spec, outs),
            scratch_shapes=scratch,
            compiler_params=params,
            name=name,
        )(*operands)

    prior = lax.ppermute(frames_in, BOTH, steps(1, 0))
    outs = [shape(frames_in.shape, frames_in.dtype), sums_shape, sums_shape, shape((8, chans), jnp.float32)]
    outs += [shape(kernel.shape, kernel.dtype)]
    outs += [shape((frames, 2, cols, chans), jnp.bfloat16)] * count
    scratch = [pltpu.SMEM((n_clip,), jnp.int32), pltpu.VMEM((6, chans), jnp.float32), pltpu.SemaphoreType.DMA((9,))]
    distant = [*args[:8], args[9]]
    frames_own, sums, match, table, kernel_one, *edges = call(
        functools.partial(first_kernel, n_clip, n_slab), outs, distant, [], scratch, "first_sums"
    )
    if n_slab == 2:
        beside = [lax.ppermute(edges[0], BOTH, steps(0, 1) + steps(0, -1))]
        corner = [lax.ppermute(edges[0], BOTH, steps(1, 1) + steps(1, -1))]
    else:
        top, bottom = edges
        beside = [lax.ppermute(bottom, BOTH, steps(0, 1)), lax.ppermute(top, BOTH, steps(0, -1))]
        corner = [lax.ppermute(bottom, BOTH, steps(1, 1)), lax.ppermute(top, BOTH, steps(1, -1))]
    sums = lax.all_to_all(sums, BOTH, 0, 0)
    hidden, sums, kernel_two = call(
        functools.partial(conv_one_kernel, n_slab),
        [shape((frames, rows + count, cols, chans), jnp.bfloat16), sums_shape, shape(kernel.shape, kernel.dtype)],
        [args[8]],
        [sums, match, table, kernel_one, frames_own, prior, *beside, *corner],
        [pltpu.VMEM((2 * frames, rows + 2 + count, cols, chans), jnp.bfloat16), pltpu.SemaphoreType.DMA((1,))],
        "conv_one",
    )
    prior = lax.ppermute(hidden, BOTH, steps(1, 0))
    sums = lax.all_to_all(sums, BOTH, 0, 0)
    return call(
        functools.partial(conv_two_kernel, n_slab),
        shape(frames_in.shape, jnp.bfloat16),
        [],
        [sums, match, table, kernel_two, hidden, prior, frames_own],
        [
            pltpu.VMEM((2 * frames, rows + 2, cols, chans), jnp.bfloat16),
            pltpu.VMEM(frames_in.shape, jnp.bfloat16),
            pltpu.SemaphoreType.DMA((frames,)),
        ],
        "conv_two",
        hbm,
    )


def solution(mesh):
    placed = (P("clip", "slab", None, None), P(), P(), P(), P(), P(), P(), P(), P(), P())
    return jax.shard_map(
        functools.partial(per_device, mesh.shape["clip"], mesh.shape["slab"]),
        mesh=mesh,
        in_specs=placed,
        out_specs=P("clip", "slab", None, None),
        check_vma=False,
    )
```

```python
import functools

import jax
import jax.numpy as jnp
from jax import lax
from jax.experimental import pallas as pl
from jax.experimental.pallas import tpu as pltpu
from jax.sharding import PartitionSpec as P


G = 32
BOTH = ("clip", "slab")
EPS = 1e-06


def moved(value, pairs):
    return lax.ppermute(value, BOTH, pairs)


def put_sums(first, second, sums_ref):
    both = jnp.concatenate([first, second], axis=0)
    sums_ref[...] = jnp.broadcast_to(both[None], sums_ref.shape)


def first_kernel(n_clip, n_slab, *refs):
    sources, refs = refs[:9], refs[9:]
    frames_ref, sums_ref, match_ref, table_ref, one_ref = refs[:5]
    edge_refs, (ids_ref, param_ref, sem) = refs[5:-3], refs[-3:]
    frames_hbm, ids_hbm, gain_one, shift_one, one_hbm, bias_one, gain_two, shift_two, bias_two = sources
    params = [gain_one, shift_one, bias_one, gain_two, shift_two, bias_two]
    copies = [
        pltpu.make_async_copy(frames_hbm, frames_ref, sem.at[0]),
        pltpu.make_async_copy(ids_hbm, ids_ref, sem.at[1]),
        pltpu.make_async_copy(one_hbm, one_ref, sem.at[2]),
    ]
    copies += [pltpu.make_async_copy(p, param_ref.at[i], sem.at[3 + i]) for i, p in enumerate(params)]
    for copy in copies:
        copy.start()
    frames, rows, cols, chans = frames_ref.shape
    slab = lax.axis_index("slab")
    position = lax.axis_index("clip")
    copies[0].wait()
    first = jnp.zeros((1, chans), jnp.float32)
    second = jnp.zeros((1, chans), jnp.float32)
    for f in range(frames):
        for r in range(rows):
            floats = frames_ref[f, r].astype(jnp.float32)
            first = first + jnp.sum(floats, axis=0, keepdims=True)
            second = second + jnp.sum(floats * floats, axis=0, keepdims=True)
    put_sums(first, second, sums_ref)
    if len(edge_refs) == 1:
        starts = [jnp.where(slab == 0, rows - 2, 0)]
    else:
        starts = [0, rows - 2]
    for edge_ref, start in zip(edge_refs, starts):
        for f in range(frames):
            for r in range(2):
                edge_ref[f, r] = frames_ref[f, start + r]
    copies[1].wait()
    own_clip = ids_ref[position]
    prior_clip = ids_ref[jnp.maximum(position - 1, 0)]
    same = jnp.logical_and(position > 0, prior_clip == own_clip).astype(jnp.float32)

    def add_block(b, blocks):
        weight = (ids_ref[b] == own_clip).astype(jnp.float32)
        for s in range(n_slab):
            match_ref[b * n_slab + s] = jnp.full((2, chans), weight, jnp.float32)
        return blocks + weight

    blocks = lax.fori_loop(0, n_clip, add_block, jnp.float32(0.0), unroll=n_clip <= 16)
    counts = blocks * float(frames * rows * n_slab * cols * (chans // G))
    for copy in copies[3:]:
        copy.wait()
    for i in range(len(params)):
        table_ref[i : i + 1] = param_ref[i : i + 1]
    table_ref[6:7] = jnp.full((1, chans), same, jnp.float32)
    table_ref[7:8] = jnp.full((1, chans), counts, jnp.float32)
    copies[2].wait()


def group_total(sums, per_group):
    lanes = lax.broadcasted_iota(jnp.int32, sums.shape, 1)
    width = 1
    while width < per_group:
        upper = pltpu.roll(sums, width, 1)
        lower = pltpu.roll(sums, sums.shape[1] - width, 1)
        sums = sums + jnp.where((lanes // width) % 2 == 0, lower, upper)
        width = 2 * width
    return sums


def half_affine(sums_ref, match_ref, table_ref, which):
    chans = table_ref.shape[1]
    total = jnp.sum(sums_ref[...] * match_ref[...], axis=0)
    moments = group_total(total, chans // G) / table_ref[7:8]
    mean, msq = moments[0:1], moments[1:2]
    scale = lax.rsqrt(msq - mean * mean + EPS) * table_ref[3 * which : 3 * which + 1]
    offset = table_ref[3 * which + 1 : 3 * which + 2] - mean * scale
    return 0.5 * scale, 0.5 * offset


def activate(raw, half_scale, half_offset):
    half = raw.astype(jnp.float32) * half_scale + half_offset
    return (half + half * jnp.tanh(half)).astype(jnp.bfloat16)


def products(act_ref, kernel_ref, frames, count, halves):
    cols, chans = act_ref.shape[2:]
    empty = jnp.zeros((chans, chans), jnp.bfloat16)

    def window(t):
        return [act_ref[t, dy : dy + count].reshape(count * cols, chans) for dy in range(3)]

    def weight(dt, dy, dx):
        return kernel_ref[dt, dy, dx] if 0 <= dt < 3 else empty

    def dot(windows, weights):
        return jnp.dot(
            jnp.concatenate(windows, axis=1), jnp.concatenate(weights, axis=0), preferred_element_type=jnp.float32
        )

    windows = [window(t) for t in range(frames + 2)]
    column = lax.broadcasted_iota(jnp.int32, (count * cols, chans), 0) % cols
    sides = [
        jnp.concatenate([weight(t - f, dy, 2) for f in range(frames)], axis=1)
        for t in range(frames + 2)
        for dy in range(3)
    ]
    pairs = [jnp.concatenate([weight(dt, dy, 0), weight(dt, dy, 1)], axis=1) for dt in range(3) for dy in range(3)]

    def finish(product, rights, f):
        left = pltpu.roll(product[:, :chans], 1, 0)
        right = pltpu.roll(rights[:, f * chans : (f + 1) * chans], count * cols - 1, 0)
        left = jnp.where(column == 0, 0.0, left)
        right = jnp.where(column == cols - 1, 0.0, right)
        return product[:, chans:] + left + right

    def main(f, part):
        return dot([w[part] for w in windows[f] + windows[f + 1] + windows[f + 2]], pairs)

    cut = (count + 1) // 2 * cols
    whole = slice(0, count * cols)
    if halves:
        mains = [jnp.concatenate([main(0, slice(0, cut)), main(0, slice(cut, count * cols))], axis=0)]
        rights = dot(sum(windows, []), sides)
        mains += [main(f, whole) for f in range(1, frames)]
    else:
        mains = [main(f, whole) for f in range(frames)]
        rights = dot(sum(windows, []), sides)
    for f in range(frames):
        yield f, finish(mains[f], rights, f)


def conv_one_kernel(n_slab, *refs):
    (two_hbm, sums_ref, match_ref, table_ref, kernel_ref, own_ref, prior_ref), refs = refs[:7], refs[7:]
    count = 1 if n_slab == 2 else 2
    beside, corner, refs = refs[:count], refs[count : 2 * count], refs[2 * count :]
    out_ref, next_sums_ref, two_ref, act_ref, sem = refs
    fetch = pltpu.make_async_copy(two_hbm, two_ref, sem.at[0])
    fetch.start()
    frames, rows, cols, chans = own_ref.shape
    out_rows = out_ref.shape[1]
    slab = lax.axis_index("slab")
    half_scale, half_offset = half_affine(sums_ref, match_ref, table_ref, 0)
    same = table_ref[6:7]
    empty = jnp.zeros((cols, chans), jnp.bfloat16)
    for at, body, borders, keep in ((0, prior_ref, corner, same), (frames, own_ref, beside, None)):
        scale = half_scale if keep is None else half_scale * keep
        offset = half_offset if keep is None else half_offset * keep
        for f in range(frames):
            if n_slab == 2:
                base = 1 + slab
                border = jnp.where(slab == 0, rows + 1, 0)
                act_ref[at + f, jnp.where(slab == 0, 0, rows + 2)] = empty
                for r in range(2):
                    act_ref[at + f, border + r] = activate(borders[0][f, r], scale, offset)
            else:
                base = 2
                has_up = (slab > 0).astype(jnp.float32)
                has_down = (slab < n_slab - 1).astype(jnp.float32)
                for r in range(2):
                    act_ref[at + f, r] = activate(borders[0][f, r], scale * has_up, offset * has_up)
                    act_ref[at + f, rows + 2 + r] = activate(borders[1][f, r], scale * has_down, offset * has_down)
            for r in range(rows):
                act_ref[at + f, base + r] = activate(body[f, r], scale, offset)
    first = jnp.zeros((1, chans), jnp.float32)
    second = jnp.zeros((1, chans), jnp.float32)
    own_base = slab if n_slab == 2 else 1
    for f, value in products(act_ref, kernel_ref, frames, out_rows, True):
        value = value + table_ref[2:3]
        value = value.reshape(out_rows, cols, chans)
        out_ref[f] = value.astype(jnp.bfloat16)
        for r in range(out_rows):
            inside = jnp.logical_and(r >= own_base, r < own_base + rows).astype(jnp.float32)
            floats = value[r]
            first = first + inside * jnp.sum(floats, axis=0, keepdims=True)
            second = second + inside * jnp.sum(floats * floats, axis=0, keepdims=True)
    put_sums(first, second, next_sums_ref)
    fetch.wait()


def conv_two_kernel(n_slab, sums_ref, match_ref, table_ref, kernel_ref, own_ref, prior_ref, residual_ref, out_hbm, act_ref, out_ref, sem):
    frames, rows, cols, chans = residual_ref.shape
    slab = lax.axis_index("slab")
    half_scale, half_offset = half_affine(sums_ref, match_ref, table_ref, 1)
    same = table_ref[6:7]
    empty = jnp.zeros((cols, chans), jnp.bfloat16)
    has_up = (slab > 0).astype(jnp.float32)
    has_down = (slab < n_slab - 1).astype(jnp.float32)
    count = own_ref.shape[1]
    stores = []
    for at, body, keep in ((0, prior_ref, same), (frames, own_ref, None)):
        scale = half_scale if keep is None else half_scale * keep
        offset = half_offset if keep is None else half_offset * keep
        for f in range(frames):
            if n_slab == 2:
                act_ref[at + f, jnp.where(slab == 0, 0, rows + 1)] = empty
                for r in range(count):
                    act_ref[at + f, 1 - slab + r] = activate(body[f, r], scale, offset)
            else:
                for r in range(count):
                    edge = has_up if r == 0 else has_down if r == count - 1 else 1.0
                    act_ref[at + f, r] = activate(body[f, r], scale * edge, offset * edge)
    for f, value in products(act_ref, kernel_ref, frames, rows, False):
        value = value + table_ref[5:6]
        value = value + residual_ref[f].reshape(rows * cols, chans).astype(jnp.float32)
        out_ref[f] = value.astype(jnp.bfloat16).reshape(rows, cols, chans)
        stores.append(pltpu.make_async_copy(out_ref.at[f], out_hbm.at[f], sem.at[f]))
        stores[-1].start()
    for store in stores:
        store.wait()


def per_device(n_clip, n_slab, *args):
    return block(n_clip, n_slab, *args)


def block(n_clip, n_slab, *args):
    frames_in, kernel = args[0], args[4]
    frames, rows, cols, chans = frames_in.shape
    count = 1 if n_slab == 2 else 2
    shape = jax.ShapeDtypeStruct
    sums_shape = shape((n_clip * n_slab, 2, chans), jnp.float32)
    vmem = pl.BlockSpec(memory_space=pltpu.VMEM)
    hbm = pl.BlockSpec(memory_space=pltpu.HBM)
    params = pltpu.CompilerParams(vmem_limit_bytes=24 << 20)

    def steps(dc, ds):
        return [
            (c * n_slab + s, (c + dc) * n_slab + s + ds)
            for c in range(n_clip - dc)
            for s in range(n_slab)
            if 0 <= s + ds < n_slab
        ]

    def call(kernel, outs, distant, operands, scratch, out_spec=vmem):
        distant = [pltpu.with_memory_space_constraint(x, pltpu.HBM) for x in distant]
        operands = distant + operands
        return pl.pallas_call(
            kernel,
            out_shape=outs,
            in_specs=[hbm] * len(distant) + [vmem] * (len(operands) - len(distant)),
            out_specs=jax.tree.map(lambda _: out_spec, outs),
            scratch_shapes=scratch,
            compiler_params=params,
        )(*operands)

    outs = [shape(frames_in.shape, frames_in.dtype), sums_shape, sums_shape, shape((8, chans), jnp.float32)]
    outs += [shape(kernel.shape, kernel.dtype)]
    outs += [shape((frames, 2, cols, chans), jnp.bfloat16)] * count
    scratch = [pltpu.SMEM((n_clip,), jnp.int32), pltpu.VMEM((6, chans), jnp.float32), pltpu.SemaphoreType.DMA((9,))]
    distant = [*args[:8], args[9]]
    frames_own, sums, match, table, kernel_one, *edges = call(
        functools.partial(first_kernel, n_clip, n_slab), outs, distant, [], scratch
    )
    if n_slab == 2:
        beside = [moved(edges[0], steps(0, 1) + steps(0, -1))]
        corner = [moved(edges[0], steps(1, 1) + steps(1, -1))]
    else:
        top, bottom = edges
        beside = [lax.ppermute(bottom, BOTH, steps(0, 1)), lax.ppermute(top, BOTH, steps(0, -1))]
        corner = [lax.ppermute(bottom, BOTH, steps(1, 1)), lax.ppermute(top, BOTH, steps(1, -1))]
    prior = moved(frames_own, steps(1, 0))
    sums = lax.all_to_all(sums, BOTH, 0, 0)
    hidden, sums, kernel_two = call(
        functools.partial(conv_one_kernel, n_slab),
        [shape((frames, rows + count, cols, chans), jnp.bfloat16), sums_shape, shape(kernel.shape, kernel.dtype)],
        [args[8]],
        [sums, match, table, kernel_one, frames_own, prior, *beside, *corner],
        [pltpu.VMEM((2 * frames, rows + 2 + count, cols, chans), jnp.bfloat16), pltpu.SemaphoreType.DMA((1,))],
    )
    prior = lax.ppermute(hidden, BOTH, steps(1, 0))
    sums = lax.all_to_all(sums, BOTH, 0, 0)
    return call(
        functools.partial(conv_two_kernel, n_slab),
        shape(frames_in.shape, jnp.bfloat16),
        [],
        [sums, match, table, kernel_two, hidden, prior, frames_own],
        [
            pltpu.VMEM((2 * frames, rows + 2, cols, chans), jnp.bfloat16),
            pltpu.VMEM(frames_in.shape, jnp.bfloat16),
            pltpu.SemaphoreType.DMA((frames,)),
        ],
        hbm,
    )


def solution(mesh):
    placed = (P("clip", "slab", None, None), P(), P(), P(), P(), P(), P(), P(), P(), P())
    return jax.shard_map(
        functools.partial(per_device, mesh.shape["clip"], mesh.shape["slab"]),
        mesh=mesh,
        in_specs=placed,
        out_specs=P("clip", "slab", None, None),
        check_vma=False,
    )
```

```python
import functools

import jax
import jax.numpy as jnp
from jax import lax
from jax.experimental import pallas as pl
from jax.experimental.pallas import tpu as pltpu
from jax.sharding import PartitionSpec as P


G = 32
BOTH = ("clip", "slab")
EPS = 1e-06


def moved(value, pairs):
    return lax.ppermute(value, BOTH, pairs)


def put_sums(first, second, sums_ref):
    totals = group_total(jnp.concatenate([first, second], axis=0), first.shape[1] // G)
    even = lax.broadcasted_iota(jnp.int32, first.shape, 1) % 2 == 0
    packed = jnp.where(even, totals[0:1], totals[1:2])
    sums_ref[...] = jnp.broadcast_to(packed[None], sums_ref.shape)


def first_kernel(n_clip, n_slab, *refs):
    sources, refs = refs[:9], refs[9:]
    frames_ref, sums_ref, match_ref, table_ref, one_ref = refs[:5]
    edge_refs, (ids_ref, param_ref, sem) = refs[5:-3], refs[-3:]
    frames_hbm, ids_hbm, gain_one, shift_one, one_hbm, bias_one, gain_two, shift_two, bias_two = sources
    params = [gain_one, shift_one, bias_one, gain_two, shift_two, bias_two]
    copies = [
        pltpu.make_async_copy(frames_hbm, frames_ref, sem.at[0]),
        pltpu.make_async_copy(ids_hbm, ids_ref, sem.at[1]),
        pltpu.make_async_copy(one_hbm, one_ref, sem.at[2]),
    ]
    copies += [pltpu.make_async_copy(p, param_ref.at[i], sem.at[3 + i]) for i, p in enumerate(params)]
    for copy in copies:
        copy.start()
    frames, rows, cols, chans = frames_ref.shape
    slab = lax.axis_index("slab")
    position = lax.axis_index("clip")
    copies[0].wait()
    first = jnp.zeros((1, chans), jnp.float32)
    second = jnp.zeros((1, chans), jnp.float32)
    for f in range(frames):
        for r in range(rows):
            floats = frames_ref[f, r].astype(jnp.float32)
            first = first + jnp.sum(floats, axis=0, keepdims=True)
            second = second + jnp.sum(floats * floats, axis=0, keepdims=True)
    put_sums(first, second, sums_ref)
    if len(edge_refs) == 1:
        starts = [jnp.where(slab == 0, rows - 2, 0)]
    else:
        starts = [0, rows - 2]
    for edge_ref, start in zip(edge_refs, starts):
        for f in range(frames):
            for r in range(2):
                edge_ref[f, r] = frames_ref[f, start + r]
    copies[1].wait()
    own_clip = ids_ref[position]
    prior_clip = ids_ref[jnp.maximum(position - 1, 0)]
    same = jnp.logical_and(position > 0, prior_clip == own_clip).astype(jnp.float32)

    def add_block(b, blocks):
        weight = (ids_ref[b] == own_clip).astype(jnp.float32)
        for s in range(n_slab):
            match_ref[b * n_slab + s] = jnp.full((1, chans), weight, jnp.float32)
        return blocks + weight

    blocks = lax.fori_loop(0, n_clip, add_block, jnp.float32(0.0), unroll=n_clip <= 16)
    counts = blocks * float(frames * rows * n_slab * cols * (chans // G))
    for copy in copies[3:]:
        copy.wait()
    for i in range(len(params)):
        table_ref[i : i + 1] = param_ref[i : i + 1]
    table_ref[6:7] = jnp.full((1, chans), same, jnp.float32)
    table_ref[7:8] = jnp.full((1, chans), counts, jnp.float32)
    copies[2].wait()


def group_total(sums, per_group):
    lanes = lax.broadcasted_iota(jnp.int32, sums.shape, 1)
    width = 1
    while width < per_group:
        upper = pltpu.roll(sums, width, 1)
        lower = pltpu.roll(sums, sums.shape[1] - width, 1)
        sums = sums + jnp.where((lanes // width) % 2 == 0, lower, upper)
        width = 2 * width
    return sums


def half_affine(sums_ref, match_ref, table_ref, which):
    chans = table_ref.shape[1]
    total = jnp.sum(sums_ref[...] * match_ref[...], axis=0)
    even = lax.broadcasted_iota(jnp.int32, total.shape, 1) % 2 == 0
    mean = jnp.where(even, total, pltpu.roll(total, 1, 1)) / table_ref[7:8]
    msq = jnp.where(even, pltpu.roll(total, chans - 1, 1), total) / table_ref[7:8]
    scale = lax.rsqrt(msq - mean * mean + EPS) * table_ref[3 * which : 3 * which + 1]
    offset = table_ref[3 * which + 1 : 3 * which + 2] - mean * scale
    return 0.5 * scale, 0.5 * offset


def activate(raw, half_scale, half_offset):
    half = raw.astype(jnp.float32) * half_scale + half_offset
    return (half + half * jnp.tanh(half)).astype(jnp.bfloat16)


def products(act_ref, kernel_ref, frames, count, halves):
    cols, chans = act_ref.shape[2:]
    empty = jnp.zeros((chans, chans), jnp.bfloat16)

    def window(t):
        return [act_ref[t, dy : dy + count].reshape(count * cols, chans) for dy in range(3)]

    def weight(dt, dy, dx):
        return kernel_ref[dt, dy, dx] if 0 <= dt < 3 else empty

    def dot(windows, weights):
        return jnp.dot(
            jnp.concatenate(windows, axis=1), jnp.concatenate(weights, axis=0), preferred_element_type=jnp.float32
        )

    windows = [window(t) for t in range(frames + 2)]
    column = lax.broadcasted_iota(jnp.int32, (count * cols, chans), 0) % cols
    sides = [
        jnp.concatenate([weight(t - f, dy, 2) for f in range(frames)], axis=1)
        for t in range(frames + 2)
        for dy in range(3)
    ]
    pairs = [jnp.concatenate([weight(dt, dy, 0), weight(dt, dy, 1)], axis=1) for dt in range(3) for dy in range(3)]

    def finish(product, rights, f):
        left = pltpu.roll(product[:, :chans], 1, 0)
        right = pltpu.roll(rights[:, f * chans : (f + 1) * chans], count * cols - 1, 0)
        left = jnp.where(column == 0, 0.0, left)
        right = jnp.where(column == cols - 1, 0.0, right)
        return product[:, chans:] + left + right

    def main(f, part):
        return dot([w[part] for w in windows[f] + windows[f + 1] + windows[f + 2]], pairs)

    cut = (count + 1) // 2 * cols
    whole = slice(0, count * cols)
    if halves:
        mains = [jnp.concatenate([main(0, slice(0, cut)), main(0, slice(cut, count * cols))], axis=0)]
        rights = dot(sum(windows, []), sides)
        mains += [main(f, whole) for f in range(1, frames)]
    else:
        mains = [main(f, whole) for f in range(frames)]
        rights = dot(sum(windows, []), sides)
    for f in range(frames):
        yield f, finish(mains[f], rights, f)


def conv_one_kernel(n_slab, *refs):
    (two_hbm, sums_ref, match_ref, table_ref, kernel_ref, own_ref, prior_ref), refs = refs[:7], refs[7:]
    count = 1 if n_slab == 2 else 2
    beside, corner, refs = refs[:count], refs[count : 2 * count], refs[2 * count :]
    out_ref, next_sums_ref, two_ref, act_ref, sem = refs
    fetch = pltpu.make_async_copy(two_hbm, two_ref, sem.at[0])
    fetch.start()
    frames, rows, cols, chans = own_ref.shape
    out_rows = out_ref.shape[1]
    slab = lax.axis_index("slab")
    half_scale, half_offset = half_affine(sums_ref, match_ref, table_ref, 0)
    same = table_ref[6:7]
    empty = jnp.zeros((cols, chans), jnp.bfloat16)
    for at, body, borders, keep in ((0, prior_ref, corner, same), (frames, own_ref, beside, None)):
        scale = half_scale if keep is None else half_scale * keep
        offset = half_offset if keep is None else half_offset * keep
        for f in range(frames):
            if n_slab == 2:
                base = 1 + slab
                border = jnp.where(slab == 0, rows + 1, 0)
                act_ref[at + f, jnp.where(slab == 0, 0, rows + 2)] = empty
                for r in range(2):
                    act_ref[at + f, border + r] = activate(borders[0][f, r], scale, offset)
            else:
                base = 2
                has_up = (slab > 0).astype(jnp.float32)
                has_down = (slab < n_slab - 1).astype(jnp.float32)
                for r in range(2):
                    act_ref[at + f, r] = activate(borders[0][f, r], scale * has_up, offset * has_up)
                    act_ref[at + f, rows + 2 + r] = activate(borders[1][f, r], scale * has_down, offset * has_down)
            for r in range(rows):
                act_ref[at + f, base + r] = activate(body[f, r], scale, offset)
    first = jnp.zeros((1, chans), jnp.float32)
    second = jnp.zeros((1, chans), jnp.float32)
    own_base = slab if n_slab == 2 else 1
    for f, value in products(act_ref, kernel_ref, frames, out_rows, True):
        value = value + table_ref[2:3]
        value = value.reshape(out_rows, cols, chans)
        out_ref[f] = value.astype(jnp.bfloat16)
        for r in range(out_rows):
            inside = jnp.logical_and(r >= own_base, r < own_base + rows).astype(jnp.float32)
            floats = value[r]
            first = first + inside * jnp.sum(floats, axis=0, keepdims=True)
            second = second + inside * jnp.sum(floats * floats, axis=0, keepdims=True)
    put_sums(first, second, next_sums_ref)
    fetch.wait()


def conv_two_kernel(n_slab, sums_ref, match_ref, table_ref, kernel_ref, own_ref, prior_ref, residual_ref, out_hbm, act_ref, out_ref, sem):
    frames, rows, cols, chans = residual_ref.shape
    slab = lax.axis_index("slab")
    half_scale, half_offset = half_affine(sums_ref, match_ref, table_ref, 1)
    same = table_ref[6:7]
    empty = jnp.zeros((cols, chans), jnp.bfloat16)
    has_up = (slab > 0).astype(jnp.float32)
    has_down = (slab < n_slab - 1).astype(jnp.float32)
    count = own_ref.shape[1]
    stores = []
    for at, body, keep in ((0, prior_ref, same), (frames, own_ref, None)):
        scale = half_scale if keep is None else half_scale * keep
        offset = half_offset if keep is None else half_offset * keep
        for f in range(frames):
            if n_slab == 2:
                act_ref[at + f, jnp.where(slab == 0, 0, rows + 1)] = empty
                for r in range(count):
                    act_ref[at + f, 1 - slab + r] = activate(body[f, r], scale, offset)
            else:
                for r in range(count):
                    edge = has_up if r == 0 else has_down if r == count - 1 else 1.0
                    act_ref[at + f, r] = activate(body[f, r], scale * edge, offset * edge)
    for f, value in products(act_ref, kernel_ref, frames, rows, False):
        value = value + table_ref[5:6]
        value = value + residual_ref[f].reshape(rows * cols, chans).astype(jnp.float32)
        out_ref[f] = value.astype(jnp.bfloat16).reshape(rows, cols, chans)
        stores.append(pltpu.make_async_copy(out_ref.at[f], out_hbm.at[f], sem.at[f]))
        stores[-1].start()
    for store in stores:
        store.wait()


def per_device(n_clip, n_slab, *args):
    return block(n_clip, n_slab, *args)


def block(n_clip, n_slab, *args):
    frames_in, kernel = args[0], args[4]
    frames, rows, cols, chans = frames_in.shape
    count = 1 if n_slab == 2 else 2
    shape = jax.ShapeDtypeStruct
    sums_shape = shape((n_clip * n_slab, 1, chans), jnp.float32)
    vmem = pl.BlockSpec(memory_space=pltpu.VMEM)
    hbm = pl.BlockSpec(memory_space=pltpu.HBM)
    params = pltpu.CompilerParams(vmem_limit_bytes=24 << 20)

    def steps(dc, ds):
        return [
            (c * n_slab + s, (c + dc) * n_slab + s + ds)
            for c in range(n_clip - dc)
            for s in range(n_slab)
            if 0 <= s + ds < n_slab
        ]

    def call(kernel, outs, distant, operands, scratch, out_spec=vmem):
        distant = [pltpu.with_memory_space_constraint(x, pltpu.HBM) for x in distant]
        operands = distant + operands
        return pl.pallas_call(
            kernel,
            out_shape=outs,
            in_specs=[hbm] * len(distant) + [vmem] * (len(operands) - len(distant)),
            out_specs=jax.tree.map(lambda _: out_spec, outs),
            scratch_shapes=scratch,
            compiler_params=params,
        )(*operands)

    outs = [shape(frames_in.shape, frames_in.dtype), sums_shape, sums_shape, shape((8, chans), jnp.float32)]
    outs += [shape(kernel.shape, kernel.dtype)]
    outs += [shape((frames, 2, cols, chans), jnp.bfloat16)] * count
    scratch = [pltpu.SMEM((n_clip,), jnp.int32), pltpu.VMEM((6, chans), jnp.float32), pltpu.SemaphoreType.DMA((9,))]
    distant = [*args[:8], args[9]]
    frames_own, sums, match, table, kernel_one, *edges = call(
        functools.partial(first_kernel, n_clip, n_slab), outs, distant, [], scratch
    )
    if n_slab == 2:
        beside = [moved(edges[0], steps(0, 1) + steps(0, -1))]
        corner = [moved(edges[0], steps(1, 1) + steps(1, -1))]
    else:
        top, bottom = edges
        beside = [lax.ppermute(bottom, BOTH, steps(0, 1)), lax.ppermute(top, BOTH, steps(0, -1))]
        corner = [lax.ppermute(bottom, BOTH, steps(1, 1)), lax.ppermute(top, BOTH, steps(1, -1))]
    prior = moved(frames_own, steps(1, 0))
    sums = lax.all_to_all(sums, BOTH, 0, 0)
    hidden, sums, kernel_two = call(
        functools.partial(conv_one_kernel, n_slab),
        [shape((frames, rows + count, cols, chans), jnp.bfloat16), sums_shape, shape(kernel.shape, kernel.dtype)],
        [args[8]],
        [sums, match, table, kernel_one, frames_own, prior, *beside, *corner],
        [pltpu.VMEM((2 * frames, rows + 2 + count, cols, chans), jnp.bfloat16), pltpu.SemaphoreType.DMA((1,))],
    )
    prior = lax.ppermute(hidden, BOTH, steps(1, 0))
    sums = lax.all_to_all(sums, BOTH, 0, 0)
    return call(
        functools.partial(conv_two_kernel, n_slab),
        shape(frames_in.shape, jnp.bfloat16),
        [],
        [sums, match, table, kernel_two, hidden, prior, frames_own],
        [
            pltpu.VMEM((2 * frames, rows + 2, cols, chans), jnp.bfloat16),
            pltpu.VMEM(frames_in.shape, jnp.bfloat16),
            pltpu.SemaphoreType.DMA((frames,)),
        ],
        hbm,
    )


def solution(mesh):
    placed = (P("clip", "slab", None, None), P(), P(), P(), P(), P(), P(), P(), P(), P())
    return jax.shard_map(
        functools.partial(per_device, mesh.shape["clip"], mesh.shape["slab"]),
        mesh=mesh,
        in_specs=placed,
        out_specs=P("clip", "slab", None, None),
        check_vma=False,
    )
```

```python
import functools

import jax
import jax.numpy as jnp
from jax import lax
from jax.experimental import pallas as pl
from jax.experimental.pallas import tpu as pltpu
from jax.sharding import PartitionSpec as P


G = 32
BOTH = ("clip", "slab")
EPS = 1e-06


def moved(value, pairs):
    return lax.ppermute(value, BOTH, pairs)


def put_sums(first, second, sums_ref):
    totals = group_total(jnp.concatenate([first, second], axis=0), first.shape[1] // G)
    even = lax.broadcasted_iota(jnp.int32, first.shape, 1) % 2 == 0
    packed = jnp.where(even, totals[0:1], totals[1:2])
    sums_ref[...] = jnp.broadcast_to(packed[None], sums_ref.shape)


def first_kernel(n_clip, n_slab, *refs):
    sources, refs = refs[:9], refs[9:]
    frames_ref, sums_ref, match_ref, table_ref, one_ref = refs[:5]
    edge_refs, (ids_ref, param_ref, sem) = refs[5:-3], refs[-3:]
    frames_hbm, ids_hbm, gain_one, shift_one, one_hbm, bias_one, gain_two, shift_two, bias_two = sources
    params = [gain_one, shift_one, bias_one, gain_two, shift_two, bias_two]
    copies = [
        pltpu.make_async_copy(frames_hbm, frames_ref, sem.at[0]),
        pltpu.make_async_copy(ids_hbm, ids_ref, sem.at[1]),
        pltpu.make_async_copy(one_hbm, one_ref, sem.at[2]),
    ]
    copies += [pltpu.make_async_copy(p, param_ref.at[i], sem.at[3 + i]) for i, p in enumerate(params)]
    for copy in copies:
        copy.start()
    frames, rows, cols, chans = frames_ref.shape
    slab = lax.axis_index("slab")
    position = lax.axis_index("clip")
    copies[0].wait()
    first = jnp.zeros((1, chans), jnp.float32)
    second = jnp.zeros((1, chans), jnp.float32)
    for f in range(frames):
        for r in range(rows):
            floats = frames_ref[f, r].astype(jnp.float32)
            first = first + jnp.sum(floats, axis=0, keepdims=True)
            second = second + jnp.sum(floats * floats, axis=0, keepdims=True)
    put_sums(first, second, sums_ref)
    if len(edge_refs) == 1:
        starts = [jnp.where(slab == 0, rows - 2, 0)]
    else:
        starts = [0, rows - 2]
    for edge_ref, start in zip(edge_refs, starts):
        for f in range(frames):
            for r in range(2):
                edge_ref[f, r] = frames_ref[f, start + r]
    copies[1].wait()
    own_clip = ids_ref[position]
    prior_clip = ids_ref[jnp.maximum(position - 1, 0)]
    same = jnp.logical_and(position > 0, prior_clip == own_clip).astype(jnp.float32)

    def add_block(b, blocks):
        weight = (ids_ref[b] == own_clip).astype(jnp.float32)
        for s in range(n_slab):
            match_ref[b * n_slab + s] = jnp.full((1, chans), weight, jnp.float32)
        return blocks + weight

    blocks = lax.fori_loop(0, n_clip, add_block, jnp.float32(0.0), unroll=n_clip <= 16)
    counts = blocks * float(frames * rows * n_slab * cols * (chans // G))
    for copy in copies[3:]:
        copy.wait()
    for i in range(len(params)):
        table_ref[i : i + 1] = param_ref[i : i + 1]
    table_ref[6:7] = jnp.full((1, chans), same, jnp.float32)
    table_ref[7:8] = jnp.full((1, chans), counts, jnp.float32)
    copies[2].wait()


def group_total(sums, per_group):
    lanes = lax.broadcasted_iota(jnp.int32, sums.shape, 1)
    width = 1
    while width < per_group:
        upper = pltpu.roll(sums, width, 1)
        lower = pltpu.roll(sums, sums.shape[1] - width, 1)
        sums = sums + jnp.where((lanes // width) % 2 == 0, lower, upper)
        width = 2 * width
    return sums


def half_affine(sums_ref, match_ref, table_ref, which):
    chans = table_ref.shape[1]
    total = jnp.sum(sums_ref[...] * match_ref[...], axis=0)
    even = lax.broadcasted_iota(jnp.int32, total.shape, 1) % 2 == 0
    mean = jnp.where(even, total, pltpu.roll(total, 1, 1)) / table_ref[7:8]
    msq = jnp.where(even, pltpu.roll(total, chans - 1, 1), total) / table_ref[7:8]
    scale = lax.rsqrt(msq - mean * mean + EPS) * table_ref[3 * which : 3 * which + 1]
    offset = table_ref[3 * which + 1 : 3 * which + 2] - mean * scale
    return 0.5 * scale, 0.5 * offset


def activate(raw, half_scale, half_offset):
    half = raw.astype(jnp.float32) * half_scale + half_offset
    return (half + half * jnp.tanh(half)).astype(jnp.bfloat16)


def products(act_ref, kernel_ref, frames, count, halves):
    cols, chans = act_ref.shape[2:]
    empty = jnp.zeros((chans, chans), jnp.bfloat16)

    def window(t):
        return [act_ref[t, dy : dy + count].reshape(count * cols, chans) for dy in range(3)]

    def weight(dt, dy, dx):
        return kernel_ref[dt, dy, dx] if 0 <= dt < 3 else empty

    def dot(windows, weights):
        return jnp.dot(
            jnp.concatenate(windows, axis=1), jnp.concatenate(weights, axis=0), preferred_element_type=jnp.float32
        )

    windows = [window(t) for t in range(frames + 2)]
    column = lax.broadcasted_iota(jnp.int32, (count * cols, chans), 0) % cols
    sides = [
        jnp.concatenate([weight(t - f, dy, 2) for f in range(frames)], axis=1)
        for t in range(frames + 2)
        for dy in range(3)
    ]
    pairs = [jnp.concatenate([weight(dt, dy, 0), weight(dt, dy, 1)], axis=1) for dt in range(3) for dy in range(3)]

    def finish(product, rights, f):
        left = pltpu.roll(product[:, :chans], 1, 0)
        right = pltpu.roll(rights[:, f * chans : (f + 1) * chans], count * cols - 1, 0)
        left = jnp.where(column == 0, 0.0, left)
        right = jnp.where(column == cols - 1, 0.0, right)
        return product[:, chans:] + left + right

    def main(f, part):
        return dot([w[part] for w in windows[f] + windows[f + 1] + windows[f + 2]], pairs)

    cut = (count + 1) // 2 * cols
    whole = slice(0, count * cols)
    if halves:
        mains = [jnp.concatenate([main(0, slice(0, cut)), main(0, slice(cut, count * cols))], axis=0)]
        rights = dot(sum(windows, []), sides)
        mains += [main(f, whole) for f in range(1, frames)]
    else:
        mains = [main(f, whole) for f in range(frames)]
        rights = dot(sum(windows, []), sides)
    for f in range(frames):
        yield f, finish(mains[f], rights, f)


def conv_one_kernel(n_slab, *refs):
    (two_hbm, sums_ref, match_ref, table_ref, kernel_ref, own_ref, prior_ref), refs = refs[:7], refs[7:]
    count = 1 if n_slab == 2 else 2
    beside, corner, refs = refs[:count], refs[count : 2 * count], refs[2 * count :]
    out_ref, next_sums_ref, two_ref, act_ref, sem = refs
    fetch = pltpu.make_async_copy(two_hbm, two_ref, sem.at[0])
    frames, rows, cols, chans = own_ref.shape
    out_rows = out_ref.shape[1]
    slab = lax.axis_index("slab")
    half_scale, half_offset = half_affine(sums_ref, match_ref, table_ref, 0)
    same = table_ref[6:7]
    empty = jnp.zeros((cols, chans), jnp.bfloat16)
    for at, body, borders, keep in ((0, prior_ref, corner, same), (frames, own_ref, beside, None)):
        scale = half_scale if keep is None else half_scale * keep
        offset = half_offset if keep is None else half_offset * keep
        for f in range(frames):
            if n_slab == 2:
                base = 1 + slab
                border = jnp.where(slab == 0, rows + 1, 0)
                act_ref[at + f, jnp.where(slab == 0, 0, rows + 2)] = empty
                for r in range(2):
                    act_ref[at + f, border + r] = activate(borders[0][f, r], scale, offset)
            else:
                base = 2
                has_up = (slab > 0).astype(jnp.float32)
                has_down = (slab < n_slab - 1).astype(jnp.float32)
                for r in range(2):
                    act_ref[at + f, r] = activate(borders[0][f, r], scale * has_up, offset * has_up)
                    act_ref[at + f, rows + 2 + r] = activate(borders[1][f, r], scale * has_down, offset * has_down)
            for r in range(rows):
                act_ref[at + f, base + r] = activate(body[f, r], scale, offset)
    fetch.start()
    first = jnp.zeros((1, chans), jnp.float32)
    second = jnp.zeros((1, chans), jnp.float32)
    own_base = slab if n_slab == 2 else 1
    for f, value in products(act_ref, kernel_ref, frames, out_rows, True):
        value = value + table_ref[2:3]
        value = value.reshape(out_rows, cols, chans)
        out_ref[f] = value.astype(jnp.bfloat16)
        for r in range(out_rows):
            inside = jnp.logical_and(r >= own_base, r < own_base + rows).astype(jnp.float32)
            floats = value[r]
            first = first + inside * jnp.sum(floats, axis=0, keepdims=True)
            second = second + inside * jnp.sum(floats * floats, axis=0, keepdims=True)
    put_sums(first, second, next_sums_ref)
    fetch.wait()


def conv_two_kernel(n_slab, sums_ref, match_ref, table_ref, kernel_ref, own_ref, prior_ref, residual_ref, out_hbm, act_ref, out_ref, sem):
    frames, rows, cols, chans = residual_ref.shape
    slab = lax.axis_index("slab")
    half_scale, half_offset = half_affine(sums_ref, match_ref, table_ref, 1)
    same = table_ref[6:7]
    empty = jnp.zeros((cols, chans), jnp.bfloat16)
    has_up = (slab > 0).astype(jnp.float32)
    has_down = (slab < n_slab - 1).astype(jnp.float32)
    count = own_ref.shape[1]
    stores = []
    for at, body, keep in ((0, prior_ref, same), (frames, own_ref, None)):
        scale = half_scale if keep is None else half_scale * keep
        offset = half_offset if keep is None else half_offset * keep
        for f in range(frames):
            if n_slab == 2:
                act_ref[at + f, jnp.where(slab == 0, 0, rows + 1)] = empty
                for r in range(count):
                    act_ref[at + f, 1 - slab + r] = activate(body[f, r], scale, offset)
            else:
                for r in range(count):
                    edge = has_up if r == 0 else has_down if r == count - 1 else 1.0
                    act_ref[at + f, r] = activate(body[f, r], scale * edge, offset * edge)
    for f, value in products(act_ref, kernel_ref, frames, rows, False):
        value = value + table_ref[5:6]
        value = value + residual_ref[f].reshape(rows * cols, chans).astype(jnp.float32)
        value = value.astype(jnp.bfloat16).reshape(rows, cols, chans)
        for part in range(2):
            piece = pl.ds(part * (rows // 2), rows // 2)
            out_ref[f, piece] = value[part * (rows // 2) : (part + 1) * (rows // 2)]
            stores.append(pltpu.make_async_copy(out_ref.at[f, piece], out_hbm.at[f, piece], sem.at[2 * f + part]))
            stores[-1].start()
    for store in stores:
        store.wait()


def per_device(n_clip, n_slab, *args):
    return block(n_clip, n_slab, *args)


def block(n_clip, n_slab, *args):
    frames_in, kernel = args[0], args[4]
    frames, rows, cols, chans = frames_in.shape
    count = 1 if n_slab == 2 else 2
    shape = jax.ShapeDtypeStruct
    sums_shape = shape((n_clip * n_slab, 1, chans), jnp.float32)
    vmem = pl.BlockSpec(memory_space=pltpu.VMEM)
    hbm = pl.BlockSpec(memory_space=pltpu.HBM)
    params = pltpu.CompilerParams(vmem_limit_bytes=24 << 20)

    def steps(dc, ds):
        return [
            (c * n_slab + s, (c + dc) * n_slab + s + ds)
            for c in range(n_clip - dc)
            for s in range(n_slab)
            if 0 <= s + ds < n_slab
        ]

    def call(kernel, outs, distant, operands, scratch, out_spec=vmem):
        distant = [pltpu.with_memory_space_constraint(x, pltpu.HBM) for x in distant]
        operands = distant + operands
        return pl.pallas_call(
            kernel,
            out_shape=outs,
            in_specs=[hbm] * len(distant) + [vmem] * (len(operands) - len(distant)),
            out_specs=jax.tree.map(lambda _: out_spec, outs),
            scratch_shapes=scratch,
            compiler_params=params,
        )(*operands)

    outs = [shape(frames_in.shape, frames_in.dtype), sums_shape, sums_shape, shape((8, chans), jnp.float32)]
    outs += [shape(kernel.shape, kernel.dtype)]
    outs += [shape((frames, 2, cols, chans), jnp.bfloat16)] * count
    scratch = [pltpu.SMEM((n_clip,), jnp.int32), pltpu.VMEM((6, chans), jnp.float32), pltpu.SemaphoreType.DMA((9,))]
    distant = [*args[:8], args[9]]
    frames_own, sums, match, table, kernel_one, *edges = call(
        functools.partial(first_kernel, n_clip, n_slab), outs, distant, [], scratch
    )
    if n_slab == 2:
        beside = [moved(edges[0], steps(0, 1) + steps(0, -1))]
        corner = [moved(edges[0], steps(1, 1) + steps(1, -1))]
    else:
        top, bottom = edges
        beside = [lax.ppermute(bottom, BOTH, steps(0, 1)), lax.ppermute(top, BOTH, steps(0, -1))]
        corner = [lax.ppermute(bottom, BOTH, steps(1, 1)), lax.ppermute(top, BOTH, steps(1, -1))]
    prior = moved(frames_own, steps(1, 0))
    sums = lax.all_to_all(sums, BOTH, 0, 0)
    hidden, sums, kernel_two = call(
        functools.partial(conv_one_kernel, n_slab),
        [shape((frames, rows + count, cols, chans), jnp.bfloat16), sums_shape, shape(kernel.shape, kernel.dtype)],
        [args[8]],
        [sums, match, table, kernel_one, frames_own, prior, *beside, *corner],
        [pltpu.VMEM((2 * frames, rows + 2 + count, cols, chans), jnp.bfloat16), pltpu.SemaphoreType.DMA((1,))],
    )
    prior = lax.ppermute(hidden, BOTH, steps(1, 0))
    sums = lax.all_to_all(sums, BOTH, 0, 0)
    return call(
        functools.partial(conv_two_kernel, n_slab),
        shape(frames_in.shape, jnp.bfloat16),
        [],
        [sums, match, table, kernel_two, hidden, prior, frames_own],
        [
            pltpu.VMEM((2 * frames, rows + 2, cols, chans), jnp.bfloat16),
            pltpu.VMEM(frames_in.shape, jnp.bfloat16),
            pltpu.SemaphoreType.DMA((2 * frames,)),
        ],
        hbm,
    )


def solution(mesh):
    placed = (P("clip", "slab", None, None), P(), P(), P(), P(), P(), P(), P(), P(), P())
    return jax.shard_map(
        functools.partial(per_device, mesh.shape["clip"], mesh.shape["slab"]),
        mesh=mesh,
        in_specs=placed,
        out_specs=P("clip", "slab", None, None),
        check_vma=False,
    )
```
